32 devices in a mesh: exp: 2 (over x), tile: 2 (over core), depth: 8 (over z, y).
Axes of the slice: x: 2, y: 2, z: 4, core: 2. Of those that a mesh axis runs over, the one named last changes fastest.
Arguments:
- images: float32 [2, 4, 256, 256], P('exp', None, 'tile'), may hold values from 0.25 to 4
- offsets: int32 [4, 64], P(None, 'depth'), may hold values from -6 to 6
- fractions: float32 [4, 64], P(None, 'depth'), may hold values from 0 to 1
- shifts: int32 [16, 3], P(('tile', 'depth')), may hold values from -8 to 7
Outputs:
- correlation: float32 [16, 64, 4096], P(('tile', 'depth'), 'exp')
The draws below stay inside these ranges and needn't reach their ends.
All inputs are finite; a program needn't handle non-finite values.
Results may differ from the reference program's by a relative error of at most 0.0003.
Values sent between devices are 32-bit elements; how exact they have to be, the bound alone decides.
No kernel may reach another device: no remote copies, remote signals or barrier semaphores. Data moves between devices by JAX's collectives and lax.ppermute only.
A program may use at most 64 MiB of HBM per device.

```python
import math
import jax
import jax.numpy as jnp
from jax import lax

CAMS = 4
BRICK = 64
ITERS = 2
NX = 256
NY = 256
NZ = 64
NBR = 16


def draw_offsets(key, part):
    slope_key = jax.random.fold_in(key, 11)
    jitter_key = jax.random.fold_in(key, 23)
    slopes = jax.random.permutation(slope_key, jnp.array([-2, -1, 1, 2], jnp.int32))
    depth_pos = jnp.arange(NZ).astype(jnp.int32)
    base = slopes[:, None] * 3 * (2 * depth_pos[None, :] - NZ + 1) // (NZ - 1)
    jitter = jax.random.randint(jitter_key, (CAMS, NZ), -1, 2).astype(jnp.int32)
    interior = ((depth_pos > 0) & (depth_pos < NZ - 1)).astype(jnp.int32)
    return jnp.clip(base + jitter * interior[None, :], -6, 6).astype(jnp.int32)


def touch_ends(drawn, own_key, smallest, largest):
    shape = drawn.shape
    spot = [jax.random.randint(jax.random.fold_in(own_key, axis), (), 0, shape[axis]) for axis in range(len(shape))]
    drawn = drawn.at[tuple(spot)].set(smallest)
    longest = shape.index(max(shape))
    spot[longest] = (spot[longest] + 1) % shape[longest]
    return drawn.at[tuple(spot)].set(largest)


def steps_of(rng, extent, cuts, low, largest):
    def one(dim, blocks):
        draws = jax.random.uniform(jax.random.fold_in(jax.random.fold_in(rng, 6), dim), (blocks,), jnp.float32, low / len(cuts), largest / len(cuts))
        return jnp.repeat(jnp.exp(draws), extent[dim] // blocks).reshape((-1,) + (1,) * (len(extent) - dim - 1))

    loudness = one(*cuts[0])
    for cut in cuts[1:]:
        loudness = loudness * one(*cut)
    return loudness


def setup_inputs(seed: int = 0) -> dict:
    streams_of = jax.random.split(jax.random.key(seed), 5)
    images = jnp.clip(jnp.exp(math.log(4.0) - 2.7725887 * jax.random.uniform(streams_of[0], (2, CAMS, NX, NY), jnp.float32) ** steps_of(streams_of[0], (2, CAMS, NX, NY), ((0, 2), (2, 2)), -0.2, 0.2)), 0.25, 4.0)
    offsets = draw_offsets(jax.random.fold_in(streams_of[4], 71), 0)
    fractions = jnp.clip(1.0 * jax.random.uniform(streams_of[2], (CAMS, NZ), jnp.float32) ** steps_of(streams_of[2], (CAMS, NZ), ((1, 8),), -0.2, 0.2), 0.0, 1.0)
    shifts = touch_ends(jax.random.randint(streams_of[3], (NBR, 3), -8, 8), jax.random.fold_in(streams_of[3], 1), -8, 7).astype(jnp.int32)
    return dict(images=images, offsets=offsets, fractions=fractions, shifts=shifts)


def tent_weights(fractions):
    tap_list = jnp.arange(-2, 4).astype(jnp.float32)
    weights = jnp.maximum(0.0, 1.0 - jnp.abs(tap_list - fractions[..., None]) / 1.5)
    return weights / jnp.sum(weights, axis=-1, keepdims=True)


def project(volume, offsets, tent):
    tap_int = jnp.arange(-2, 4).astype(jnp.int32)
    columns = jnp.arange(NX).astype(jnp.int32)

    def z_step(total, depth_index):
        index_map = jnp.mod(columns[None, None, :] - offsets[:, depth_index][:, None, None] - tap_int[None, :, None], NX)
        gathered = jnp.take(volume[depth_index], index_map, axis=0)
        total = total + jnp.sum(tent[:, depth_index, :, None, None] * gathered, axis=1)
        return total, None

    start = jnp.zeros((CAMS, NX, NY), jnp.float32)
    total, _ = lax.scan(z_step, start, jnp.arange(NZ).astype(jnp.int32))
    return total / NZ


def backproject(ratio, offsets, tent):
    tap_int = jnp.arange(-2, 4).astype(jnp.int32)
    columns = jnp.arange(NX).astype(jnp.int32)
    cameras = jnp.arange(CAMS).astype(jnp.int32)

    def per_slab(depth_index):
        index_map = jnp.mod(columns[None, None, :] + offsets[:, depth_index][:, None, None] + tap_int[None, :, None], NX)
        gathered = ratio[cameras[:, None, None], index_map]
        return jnp.sum(tent[:, depth_index, :, None, None] * gathered, axis=(0, 1)) / CAMS

    return lax.map(per_slab, jnp.arange(NZ).astype(jnp.int32))


def reconstruct(image_set, offsets, tent):
    log_images = jnp.log(image_set)
    log_volume = jnp.zeros((NZ, NX, NY), jnp.float32)
    for iteration in range(ITERS):
        volume = jnp.exp(log_volume)
        ratio = log_images - jnp.log(project(volume, offsets, tent))
        log_volume = log_volume + backproject(ratio, offsets, tent)
    return jnp.exp(log_volume)


def to_bricks(volume):
    shaped = volume.reshape(NZ, NX // BRICK, BRICK, NY // BRICK, BRICK)
    return shaped.transpose(1, 3, 0, 2, 4).reshape(-1, BRICK, BRICK, BRICK)


def reference(images, offsets, fractions, shifts):
    tent = tent_weights(fractions)
    first = to_bricks(reconstruct(images[0], offsets, tent))
    second = to_bricks(reconstruct(images[1], offsets, tent))
    wave = jnp.arange(BRICK).astype(jnp.int32)

    def per_brick(inputs):
        brick_one, brick_two, shift_row = inputs
        spec_one = jnp.fft.fftn(brick_one, norm="ortho")
        spec_two = jnp.fft.fftn(brick_two, norm="ortho")
        turns = (wave[:, None, None] * shift_row[0] + wave[None, :, None] * shift_row[1] + wave[None, None, :] * shift_row[2]) % BRICK
        angle = turns.astype(jnp.float32) * (2.0 * math.pi / BRICK)
        scale = jnp.maximum(jnp.abs(spec_one) * jnp.abs(spec_two), 0.01)
        cross = jnp.conj(spec_one) * spec_two * (jnp.cos(angle) + 1j * jnp.sin(angle)) / scale
        anchor = (wave[:, None, None] == 0) & (wave[None, :, None] == 0) & (wave[None, None, :] == 0)
        cross = jnp.where(anchor, jnp.zeros_like(cross), cross)
        result = jnp.real(jnp.fft.ifftn(cross, norm="ortho"))
        return result.reshape(BRICK, BRICK * BRICK).astype(jnp.float32)

    return lax.map(per_brick, (first, second, shifts))
```

```python
import math

import jax
import jax.numpy as jnp
from jax import lax
from jax.sharding import PartitionSpec as P

BRICK = 64
MARGIN = 32
SHIFT_LOW = -8
PAIRS = 9
highest = lax.Precision.HIGHEST
spectral_floor = 0.01


def tent_value(distance, fraction):
    return jnp.maximum(0.0, 1.0 - jnp.abs(distance - fraction) / 1.5)


def share_tables(offsets, fractions):
    both = jnp.stack([offsets.astype(jnp.float32), fractions])
    count = lax.axis_size("depth")
    sent = jnp.broadcast_to(both[None], (count,) + both.shape)
    got = lax.all_to_all(sent, "depth", split_axis=0, concat_axis=0, tiled=True)
    got = got.transpose(1, 2, 0, 3).reshape(2, both.shape[1], -1)
    return got[0], got[1]


def windows(images, bricks_x, bricks_y):
    exps, tiles, depths = (lax.axis_size(a) for a in ("exp", "tile", "depth"))
    depth_index = lax.axis_index("depth")
    part = depth_index // bricks_y
    width = images.shape[2]
    strip = lax.dynamic_slice_in_dim(images[0], depth_index % bricks_y * BRICK, BRICK, axis=2)

    def linear(e, t, d):
        return (e * tiles + t % tiles) * depths + d

    def edge(step, first, other):
        edge_part = 0 if step == 1 else bricks_x - 1
        return [
            (linear(e, t, d), linear((e + other) % exps, t + step, d))
            for e in range(exps)
            for t in range(tiles)
            for d in range(depths)
            if d // bricks_y == edge_part
        ]

    axes = ("exp", "tile", "depth")
    tail = strip[:, width - MARGIN :]
    head = strip[:, :MARGIN]
    if bricks_x > 1:
        sent = jnp.where(part == 0, tail, head)
        pads = []
        for other in (0, 1):
            got = lax.ppermute(sent, axes, edge(1, 0, other) + edge(-1, 0, other))
            pads.append((got, got))
    else:
        pads = [
            (lax.ppermute(tail, axes, edge(1, 0, other)), lax.ppermute(head, axes, edge(-1, 0, other)))
            for other in (0, 1)
        ]
    other_strip = lax.ppermute(strip, "exp", [(i, (i + 1) % exps) for i in range(exps)])
    out = []
    for (left, right), mid in zip(pads, (strip, other_strip)):
        wide = jnp.concatenate([left, mid, right], axis=1)
        out.append(lax.dynamic_slice_in_dim(wide, part * BRICK, BRICK + 2 * MARGIN, axis=1))
    return out


def weight_table(offsets, fractions):
    taps = jnp.arange(-2, 4).astype(jnp.float32)
    total = jnp.sum(tent_value(taps, fractions[..., None]), axis=-1)
    cams, slabs = offsets.shape
    shift = (SHIFT_LOW + jnp.arange(2 * PAIRS)).astype(jnp.float32)
    w = tent_value(shift[None, :, None] - offsets.T[:, None, :], fractions.T[:, None, :]) / total.T[:, None, :]
    return w.reshape(slabs, 2 * PAIRS * cams)


def reconstruct(logs, table, cams):
    slabs = table.shape[0]

    def spread(rows, first, count):
        return jnp.concatenate([rows[:, first + 128 * q : first + 128 * q + count] for q in range(PAIRS)], axis=0)

    def both(rows):
        return jnp.concatenate([rows, jnp.roll(rows, -BRICK, axis=1)], axis=0)

    dot = lambda a, b: jnp.dot(a, b, precision=highest, preferred_element_type=jnp.float32)
    uniform = jnp.sum(table, axis=0).reshape(2 * PAIRS, cams).sum(0) / slabs
    first_ratio = logs - jnp.log(uniform)[:, None]
    lo, hi = -18, BRICK + 18
    volume = jnp.exp(dot(table / cams, spread(both(first_ratio), (lo + SHIFT_LOW + MARGIN) * BRICK, (hi - lo) * BRICK)))
    q_rows = dot(table.T / slabs, volume)
    ulo, uhi = -10, BRICK + 10
    count = (uhi - ulo) * BRICK
    pair_sum = sum(
        q_rows[2 * cams * q : 2 * cams * (q + 1), (ulo - SHIFT_LOW - 2 * q - lo) * BRICK :][:, :count] for q in range(PAIRS)
    )
    proj = pair_sum[:cams, 2 * BRICK :] + pair_sum[cams:, BRICK : count - BRICK]
    second_ratio = logs[:, (ulo + 2 + MARGIN) * BRICK : (uhi + MARGIN) * BRICK] - jnp.log(proj)
    ratio = first_ratio[:, (ulo + 2 + MARGIN) * BRICK : (uhi + MARGIN) * BRICK] + second_ratio
    return jnp.exp(dot(table / cams, spread(both(ratio), 0, BRICK * BRICK)))


def dft(length):
    wave = jnp.arange(length, dtype=jnp.int32)
    angle = (wave[:, None] * wave[None, :] % length).astype(jnp.float32) * (2.0 * math.pi / length)
    return jnp.cos(angle) / math.sqrt(length), jnp.sin(angle) / math.sqrt(length)


def correlate(vol_own, vol_other, shift, exp_index):
    n = BRICK
    half = n // 2 + 1
    planes = n // 2
    cos_t, sin_t = dft(n)
    ein = lambda s, *a: jnp.einsum(s, *a, precision=highest, preferred_element_type=jnp.float32)
    vols = jnp.stack([vol_own, vol_other]).reshape(2, n, n, n)
    zt = jnp.stack([cos_t[:half], -sin_t[:half]])
    s = ein("rkz,ezxy->rekxy", zt, vols)

    def complex_dot(spec, pair, c, sn):
        a = ein(spec, pair[0], c), ein(spec, pair[0], sn), ein(spec, pair[1], c), ein(spec, pair[1], sn)
        return a[0] - a[3], a[1] + a[2]

    s = complex_dot("ekxy,yl->ekxl", s, cos_t, -sin_t)
    s = complex_dot("ekxl,xm->ekml", s, cos_t, -sin_t)
    re, im = s
    p_re = re[0] * re[1] + im[0] * im[1]
    p_im = (re[0] * im[1] - im[0] * re[1]) * (1.0 - 2.0 * exp_index.astype(jnp.float32))
    power = (re[0] * re[0] + im[0] * im[0]) * (re[1] * re[1] + im[1] * im[1])
    gain = 1.0 / jnp.maximum(jnp.sqrt(power), spectral_floor)
    kz, kx, ky = (lax.broadcasted_iota(jnp.int32, gain.shape, d) for d in range(3))
    gain = jnp.where((kz == 0) & (kx == 0) & (ky == 0), 0.0, gain)
    cross = (p_re * gain, p_im * gain)
    rows = lambda t, by: lax.dynamic_slice_in_dim(jnp.concatenate([t, t]), by % n, n, 0)
    turn = [(rows(cos_t, shift[i]), rows(sin_t, shift[i])) for i in range(3)]
    cross = complex_dot("kml,xm->kxl", cross, *turn[1])
    cross = complex_dot("kxl,yl->kxy", cross, *turn[2])
    double = jnp.where((jnp.arange(half) == 0) | (jnp.arange(half) == planes), 1.0, 2.0)
    cz, sz = (lax.dynamic_slice_in_dim(t, exp_index * planes, planes, 0)[:, :half] * double for t in turn[0])
    return ein("zk,kxy->zxy", cz, cross[0]) - ein("zk,kxy->zxy", sz, cross[1])


def per_device(images, offsets, fractions, shifts):
    cams, width, rows_y = images.shape[1:]
    bricks_x, bricks_y = width // BRICK, rows_y // BRICK
    all_off, all_frac = share_tables(offsets, fractions)
    table = weight_table(all_off, all_frac)
    vols = [
        reconstruct(jnp.log(w).reshape(cams, -1), table, cams) for w in windows(images, bricks_x, bricks_y)
    ]
    out = correlate(vols[0], vols[1], shifts[0], lax.axis_index("exp"))
    return out.reshape(1, BRICK // 2, BRICK * BRICK)


def solution(mesh):
    placed = (
        P("exp", None, "tile", None),
        P(None, "depth"),
        P(None, "depth"),
        P(("tile", "depth"), None),
    )
    return jax.shard_map(
        per_device,
        mesh=mesh,
        in_specs=placed,
        out_specs=P(("tile", "depth"), "exp", None),
        check_vma=False,
    )
```

```python
import functools
import math

import jax
import jax.numpy as jnp
import numpy as np
from jax import lax
from jax.experimental import pallas as pl
from jax.experimental.pallas import tpu as pltpu
from jax.sharding import PartitionSpec as P

BRICK = 64
HALF = BRICK // 2
ROWS = 40
MARGIN = 32
SHIFT_LOW = -8
PAIRS = 9
REACH = 18
KZ_STEPS = 6
KZ_PER_STEP = 6
spectral_floor = 0.01
f32, bf16 = jnp.float32, jnp.bfloat16


def split(value):
    high = value.astype(bf16)
    return high, (value - high.astype(f32)).astype(bf16)


def dot(a, b):
    return jnp.dot(a, b, preferred_element_type=f32)


def tent_value(distance, fraction):
    return jnp.maximum(0.0, 1.0 - jnp.abs(distance - fraction) / 1.5)


def dft_parts():
    wave = np.arange(BRICK)
    angle = (wave[:, None] * wave[None, :] % BRICK) * (2.0 * math.pi / BRICK)
    return np.cos(angle) / math.sqrt(BRICK), np.sin(angle) / math.sqrt(BRICK)


def host_split(value):
    high = value.astype(np.float32).astype(bf16)
    return high, (value - high.astype(np.float64)).astype(np.float32).astype(bf16)


def constant_tables():
    c, s = dft_parts()
    n = BRICK
    zt = np.zeros((2 * ROWS, n))
    zt[: HALF + 1], zt[ROWS : ROWS + HALF + 1] = c[: HALF + 1], -s[: HALF + 1]
    high, low = host_split(zt)
    z_fwd = np.concatenate([high, high, low], axis=1)
    yt = np.zeros((2, 2, n, 2, 2, n))
    for p in range(2):
        yt[0, p, :, p, 0], yt[0, p, :, p, 1] = c, -s
        yt[1, p, :, p, 0], yt[1, p, :, p, 1] = s, c
    high, low = host_split(yt.reshape(4 * n, 4 * n))
    y_fwd = np.concatenate([high, high, low], axis=0)
    order = np.concatenate([np.arange(0, n, 2), np.arange(1, n, 2)])
    high, low = host_split(np.concatenate([c[:, order], s[:, order]], axis=1))
    x_fwd = np.concatenate([np.concatenate([high, high], 1), np.concatenate([low, low], 1)], 0)
    twice = lambda t: np.concatenate([t, t], axis=0)
    x_inv = twice(np.concatenate([c, -s], axis=1)).astype(np.float32)
    y_inv = np.stack([np.concatenate([twice(c), twice(-s)], 1).T, np.concatenate([twice(s), twice(c)], 1).T])
    y_inv = y_inv.astype(np.float32)
    weight = np.full(ROWS, 2.0)
    weight[0] = weight[HALF] = 1.0
    weight[HALF + 1 :] = 0.0
    third = lambda t: np.pad(np.tile(t[:, :ROWS] * weight, (1, 3)), ((0, 0), (0, 2 * n - 3 * ROWS)))
    z_inv = np.stack([twice(third(c)), twice(third(-s))]).astype(np.float32)
    return z_fwd, y_fwd, x_fwd, x_inv, y_inv, z_inv


def kernel(
    shift_ref, own_ref, other_ref, pad_own_ref, pad_other_ref, tab_ref,
    z_fwd_ref, y_fwd_ref, x_fwd_ref, x_inv_ref, y_inv_ref, z_inv_ref,
    out_ref,
    raw_ref, log_ref, pack_ref, high_ref, shifted_ref, spec_ref, line_ref,
    back_ref, forward_ref, xi_ref, yi_ref, zi_ref,
    *, bricks_y,
):
    n = BRICK
    exp_index = lax.axis_index("exp")
    part = lax.axis_index("depth") // bricks_y
    window = (n + 2 * MARGIN) * n
    pad = MARGIN * n
    strip = own_ref.shape[1]

    tab = tab_ref[...]
    rows = lax.broadcasted_iota(jnp.int32, (8, 2 * n), 0)
    offs = jnp.where(rows < 4, tab, pltpu.roll(tab, 4, 0))
    frac = jnp.where(rows < 4, pltpu.roll(tab, 4, 0), tab)
    total = sum(tent_value(float(d), frac) for d in range(-2, 4))
    parity = (rows >= 4).astype(f32)
    blocks = [tent_value(SHIFT_LOW + 2 * q + parity - offs, frac) / total for q in range(PAIRS)]
    sums = jnp.sum(sum(blocks)[:, :n], axis=1, keepdims=True) / n
    uniform = jnp.log(sums + pltpu.roll(jnp.broadcast_to(sums, (8, 2 * n)), 4, 0)[:, :1])
    both_high, back_low = [], []
    for block in blocks:
        high, low = split(block / 4.0)
        both_high += [high.astype(f32)] * 2
        back_low.append(low.astype(f32))
    stacked = jnp.concatenate(both_high + back_low + [jnp.zeros((40, 2 * n), f32)], axis=0)
    back_ref[...] = jnp.transpose(stacked)[:n, :224].astype(bf16)
    high, low = split(jnp.concatenate(blocks, axis=0) / n)
    forward_ref[...] = jnp.concatenate([high, low], axis=1)[:, : 3 * n]

    sz, sx, sy = (shift_ref[0, i] + n for i in range(3))
    high, low = split(x_inv_ref[pl.ds(lax.rem(sx, n), n), :])
    xi_ref[0:n, 0 : 2 * n] = high
    xi_ref[0:n, 2 * n :] = high
    xi_ref[n:, 0 : 2 * n] = low
    xi_ref[n:, 2 * n :] = low
    lane = lax.broadcasted_iota(jnp.int32, (2 * n, 2 * n), 1)
    back = lax.rem(2 * n - lax.rem(sy, n), 2 * n)
    turned = jnp.where(lane < n, pltpu.roll(y_inv_ref[0], back, 1), pltpu.roll(y_inv_ref[1], back, 1))
    high, low = split(turned)
    yi_ref[0 : 2 * n, 0 : 2 * n] = high
    yi_ref[2 * n :, 0 : 2 * n] = high
    yi_ref[0 : 2 * n, 2 * n :] = low
    yi_ref[2 * n :, 2 * n :] = low
    first = lax.rem(HALF * exp_index + sz, n)
    turned = jnp.concatenate([z_inv_ref[0, pl.ds(first, HALF), :], z_inv_ref[1, pl.ds(first, HALF), :]], axis=0)
    high, low = split(turned)
    col = lax.broadcasted_iota(jnp.int32, turned.shape, 1)
    zi_ref[...] = jnp.where(col < 2 * ROWS, high.astype(f32), low.astype(f32)).astype(bf16)

    def spread(e, first_lane, count):
        pieces = [pack_ref[e, :, pl.ds(first_lane + 128 * q, count)] for q in range(PAIRS)]
        pieces += [high_ref[e, :, pl.ds(first_lane + 128 * q, count)] for q in range(0, PAIRS, 2)]
        return jnp.concatenate(pieces, axis=0)

    def pack(e, ratio):
        lanes = ratio.shape[1]
        row = lax.broadcasted_iota(jnp.int32, ratio.shape, 0)
        both = jnp.where(row < 4, ratio, pltpu.roll(pltpu.roll(ratio, 4, 0), lanes - n, 1))
        high = both.astype(bf16).astype(f32)
        pack_ref[e, :, 0:lanes] = jnp.concatenate([high, both - high], axis=0).astype(bf16)
        high_ref[e, :, 0:lanes] = jnp.concatenate([high, pltpu.roll(high, lanes - 128, 1)], axis=0).astype(bf16)

    for e, (strip_ref, pad_ref) in enumerate(((own_ref, pad_own_ref), (other_ref, pad_other_ref))):
        raw_ref[e, 0:4, 0:pad] = pad_ref[0]
        raw_ref[e, 0:4, pad : pad + strip] = strip_ref[...]
        raw_ref[e, 0:4, pad + strip :] = pad_ref[pad_ref.shape[0] - 1]
        raw_ref[e, 4:8, :] = jnp.ones((4, strip + 2 * pad), f32)
    for e in range(2):
        logs = jnp.log(raw_ref[e, :, pl.ds(pl.multiple_of(part * (n * n), n * n), window)])
        log_ref[e] = logs
        pack(e, logs - uniform)

    lo_x, hi_x = -REACH, n + REACH
    chunk = 1280
    back_w = back_ref[...]
    forward_w = forward_ref[...]

    def first_pass(i, _):
        start = pl.multiple_of(i * chunk, 256)
        for e in range(2):
            logv = dot(back_w, spread(e, start + (lo_x + SHIFT_LOW + MARGIN) * n, chunk))
            high, low = split(jnp.exp(logv))
            shifted_ref[e, :, pl.ds(start, chunk)] = dot(forward_w, jnp.concatenate([high, low, high], axis=0))
        return 0

    lax.fori_loop(0, (hi_x - lo_x) * n // chunk, first_pass, 0)

    lo_u, hi_u = -10, n + 10
    count = (hi_u - lo_u) * n
    for e in range(2):
        gathered = sum(
            shifted_ref[e, 8 * q : 8 * q + 8, (lo_u - SHIFT_LOW - 2 * q - lo_x) * n :][:, :count] for q in range(PAIRS)
        )
        proj = gathered + pltpu.roll(pltpu.roll(gathered, n, 1), 4, 0)
        logs = log_ref[e, :, (lo_u + 2 + MARGIN) * n : (hi_u + MARGIN) * n]
        second = logs - jnp.log(proj[:, 2 * n :])
        pack(e, (logs - uniform) + second)

    chunk2 = 1024
    per = chunk2 // (2 * n)

    def second_pass(i, _):
        start = pl.multiple_of(i * chunk2, chunk2)
        for e in range(2):
            logv = dot(back_w, spread(e, start, chunk2))
            high, low = split(jnp.exp(logv))
            spec = dot(z_fwd_ref[...], jnp.concatenate([high, low, high], axis=0))
            groups = []
            for j in range(per):
                piece = spec[:, 2 * n * j : 2 * n * (j + 1)]
                groups.append(jnp.concatenate([piece[:ROWS], piece[ROWS:]], axis=1))
            high, low = split(jnp.concatenate(groups, axis=0))
            lines = dot(jnp.concatenate([high, low, high], axis=1), y_fwd_ref[...])
            at = pl.multiple_of(i * (per * ROWS), per * ROWS)
            spec_ref[e, 0, pl.ds(at, per * ROWS), :] = lines[:, : 2 * n]
            spec_ref[e, 1, pl.ds(at, per * ROWS), :] = lines[:, 2 * n :]
        return 0

    lax.fori_loop(0, n * n // chunk2, second_pass, 0)

    lane = lax.broadcasted_iota(jnp.int32, (n, 2 * n), 1)
    row = lax.broadcasted_iota(jnp.int32, (n, 2 * n), 0)
    swap_sign = jnp.where(lane < n, 1.0, -1.0)
    exp_sign = jnp.where(lane < n, 1.0, jnp.where(exp_index == 0, 1.0, -1.0))
    anchor = ((lane % n) == 0) & (row == 0)
    swap = lambda v: pltpu.roll(v, n, 1)

    def stack(pieces):
        value = jnp.concatenate(pieces, axis=1)
        turned = jnp.concatenate([swap(v) * swap_sign for v in pieces], axis=1)
        high, low = split(jnp.concatenate([value, turned], axis=0))
        return jnp.concatenate([high, low], axis=0)

    def spectra(i, _):
        for pair in range(KZ_PER_STEP // 2):
            crosses = []
            for odd in range(2):
                kz = i * KZ_PER_STEP + 2 * pair + odd
                lines = [
                    jnp.concatenate([spec_ref[e, p, pl.ds(kz, HALF, stride=ROWS), :] for p in range(2)], axis=0)
                    for e in range(2)
                ]
                both = dot(x_fwd_ref[...], stack(lines))
                both = both[:n] + both[n:]
                one, two = both[:, : 2 * n], both[:, 2 * n :]
                power_one, power_two = one * one, two * two
                power = (power_one + swap(power_one)) * (power_two + swap(power_two))
                gain = lax.rsqrt(jnp.maximum(power, spectral_floor * spectral_floor))
                direct = one * two
                mixed = one * swap(two)
                cross = jnp.where(lane < n, direct + swap(direct), swap(mixed) - mixed) * (gain * exp_sign)
                crosses.append(jnp.where(anchor & (kz == 0), 0.0, cross))
            rows_x = dot(xi_ref[...], stack(crosses))
            rows_x = rows_x[:n] + rows_x[n:]
            high, low = split(jnp.concatenate([rows_x[:, : 2 * n], rows_x[:, 2 * n :]], axis=0))
            lines = dot(jnp.concatenate([high, low], axis=1), yi_ref[...])
            at = pl.multiple_of((i * KZ_PER_STEP + 2 * pair) * n, 2 * n)
            line_ref[pl.ds(at, 2 * n), :] = lines[:, : 2 * n] + lines[:, 2 * n :]
        return 0

    lax.fori_loop(0, KZ_STEPS, spectra, 0)
    done = KZ_STEPS * KZ_PER_STEP
    line_ref[done * n :, :] = jnp.zeros(((ROWS - done) * n, 2 * n), f32)

    pad_rows = jnp.zeros((2 * n - 3 * ROWS, 4 * n), f32)
    lane = lax.broadcasted_iota(jnp.int32, (HALF, 2 * n), 1)
    x_per_step = 8

    def planes(i, _):
        for t in range(x_per_step):
            pair = i * x_per_step + t
            cols = jnp.concatenate([line_ref[pl.ds(2 * pair + p, ROWS, stride=n), :] for p in range(2)], axis=1)
            high = cols.astype(bf16).astype(f32)
            weights = jnp.concatenate([high, cols - high, high, pad_rows], axis=0).astype(bf16)
            both = dot(zi_ref[...], weights)
            cos_part, sin_part = both[:HALF], both[HALF:]
            even_c, odd_c = cos_part[:, : 2 * n], cos_part[:, 2 * n :]
            even_s, odd_s = sin_part[:, : 2 * n], sin_part[:, 2 * n :]
            value = jnp.where(lane < n, even_c, odd_s) + swap(jnp.where(lane < n, odd_c, even_s))
            out_ref[:, pl.ds(pl.multiple_of(pair * 2 * n, 2 * n), 2 * n)] = value
        return 0

    lax.fori_loop(0, HALF // x_per_step, planes, 0)


def share_tables(offsets, fractions):
    both = jnp.concatenate([offsets.astype(f32), fractions], axis=0)
    count = lax.axis_size("depth")
    slab = both.shape[1]
    lane = jnp.arange(2 * count * slab, dtype=jnp.int32) % (count * slab)
    mine = (lane // slab == lax.axis_index("depth")).astype(f32)
    table = jnp.tile(both, (1, 2 * count)) * mine
    step = 1
    while step < count:
        table = table + lax.ppermute(table, "depth", [(i, i ^ step) for i in range(count)])
        step *= 2
    return table


def windows(images, bricks_x, bricks_y):
    exps, tiles, depths = (lax.axis_size(a) for a in ("exp", "tile", "depth"))
    depth_index = lax.axis_index("depth")
    cams = images.shape[1]
    strip = lax.dynamic_slice_in_dim(images[0], depth_index % bricks_y * BRICK, BRICK, axis=2).reshape(cams, -1)

    def linear(e, t, d):
        return ((e % exps) * tiles + t % tiles) * depths + d

    def edge(step, other):
        edge_part = 0 if step == 1 else bricks_x - 1
        return [
            (linear(e, t, d), linear(e + other, t + step, d))
            for e in range(exps)
            for t in range(tiles)
            for d in range(depths)
            if d // bricks_y == edge_part
        ]

    axes = ("exp", "tile", "depth")
    tail = strip[:, -MARGIN * BRICK :]
    head = strip[:, : MARGIN * BRICK]
    pads = []
    for other in (0, 1):
        if bricks_x > 1:
            sent = jnp.where(depth_index // bricks_y == 0, tail, head)
            pads.append(lax.ppermute(sent, axes, edge(1, other) + edge(-1, other))[None])
        else:
            pads.append(jnp.stack([lax.ppermute(tail, axes, edge(1, other)), lax.ppermute(head, axes, edge(-1, other))]))
    other_strip = lax.ppermute(strip, "exp", [(i, (i + 1) % exps) for i in range(exps)])
    return strip, other_strip, pads[0], pads[1]


def per_device(images, offsets, fractions, shifts):
    cams, width, rows_y = images.shape[1:]
    bricks_x, bricks_y = width // BRICK, rows_y // BRICK
    assert cams == 4 and width % BRICK == 0 and rows_y % BRICK == 0
    assert bricks_x * bricks_y == lax.axis_size("depth")
    assert offsets.shape[1] * lax.axis_size("depth") == BRICK
    n = BRICK
    table = share_tables(offsets, fractions)
    strips = windows(images, bricks_x, bricks_y)
    window = (n + 2 * MARGIN) * n
    extended = (width + 2 * MARGIN) * n
    vmem = pl.BlockSpec(memory_space=pltpu.VMEM)
    out = pl.pallas_call(
        functools.partial(kernel, bricks_y=bricks_y),
        out_shape=jax.ShapeDtypeStruct((HALF, n * n), f32),
        in_specs=[pl.BlockSpec(memory_space=pltpu.SMEM)] + [vmem] * 11,
        out_specs=vmem,
        scratch_shapes=[
            pltpu.VMEM((2, 8, extended), f32),
            pltpu.VMEM((2, 8, window), f32),
            pltpu.VMEM((2, 16, window), bf16),
            pltpu.VMEM((2, 16, window), bf16),
            pltpu.VMEM((2, 8 * PAIRS, (n + 2 * REACH) * n), f32),
            pltpu.VMEM((2, 2, HALF * ROWS, 2 * n), f32),
            pltpu.VMEM((ROWS * n, 2 * n), f32),
            pltpu.VMEM((n, 224), bf16),
            pltpu.VMEM((8 * PAIRS, 3 * n), bf16),
            pltpu.VMEM((2 * n, 4 * n), bf16),
            pltpu.VMEM((4 * n, 4 * n), bf16),
            pltpu.VMEM((n, 2 * n), bf16),
        ],
        compiler_params=pltpu.CompilerParams(vmem_limit_bytes=40 * 1024 * 1024),
    )(shifts, *strips, table, *(jnp.asarray(t) for t in constant_tables()))
    return out.reshape(1, HALF, n * n)


def solution(mesh):
    placed = (
        P("exp", None, "tile", None),
        P(None, "depth"),
        P(None, "depth"),
        P(("tile", "depth"), None),
    )
    return jax.shard_map(
        per_device,
        mesh=mesh,
        in_specs=placed,
        out_specs=P(("tile", "depth"), "exp", None),
        check_vma=False,
    )
```

```python
import functools
import math

import jax
import jax.numpy as jnp
import numpy as np
from jax import lax
from jax.experimental import pallas as pl
from jax.experimental.pallas import tpu as pltpu
from jax.sharding import PartitionSpec as P

BRICK = 64
HALF = BRICK // 2
ROWS = 40
MARGIN = 32
SHIFT_LOW = -8
PAIRS = 9
REACH = 18
UNROLL = 2
STEPS = 9
GROUPS = 24
GAP = 72
spectral_floor = 0.01
f32, bf16 = jnp.float32, jnp.bfloat16


def split(value):
    high = value.astype(bf16)
    return high, (value - high.astype(f32)).astype(bf16)


def dot(a, b):
    return jnp.dot(a, b, preferred_element_type=f32)


def tent_value(distance, fraction):
    return jnp.maximum(0.0, 1.0 - jnp.abs(distance - fraction) / 1.5)


def dft_parts():
    wave = np.arange(BRICK)
    angle = (wave[:, None] * wave[None, :] % BRICK) * (2.0 * math.pi / BRICK)
    return np.cos(angle) / math.sqrt(BRICK), np.sin(angle) / math.sqrt(BRICK)


def host_split(value):
    high = value.astype(np.float32).astype(bf16)
    return high, (value - high.astype(np.float64)).astype(np.float32).astype(bf16)


def constant_tables():
    c, s = dft_parts()
    n = BRICK
    zt = np.zeros((2 * ROWS, n))
    zt[: HALF + 1], zt[ROWS : ROWS + HALF + 1] = c[: HALF + 1], -s[: HALF + 1]
    high, low = host_split(zt)
    z_fwd = np.concatenate([high, high, low], axis=1)
    yt = np.zeros((2, 2, n, 2, 2, n))
    for e in range(2):
        yt[0, e, :, 0, e], yt[0, e, :, 1, e] = c, -s
        yt[1, e, :, 0, e], yt[1, e, :, 1, e] = s, c
    high, low = host_split(yt.reshape(4 * n, 4 * n))
    y_fwd = np.concatenate([high, high, low], axis=0)
    high, low = host_split(np.concatenate([c, s], axis=0))
    x_fwd = np.concatenate([high, high, low], axis=1)
    twice = lambda t: np.concatenate([t, t], axis=0)
    x_inv = np.stack([np.tile(twice(t), (1, 2)) for t in (c, s)]).astype(np.float32)
    y_inv = np.stack([np.concatenate([twice(c), twice(-s)], 1).T, np.concatenate([twice(s), twice(c)], 1).T])
    y_inv = y_inv.astype(np.float32)
    weight = np.zeros(2 * GROUPS)
    weight[: HALF + 1] = 2.0
    weight[0] = weight[HALF] = 1.0
    z_inv = []
    for odd in range(2):
        pick = np.concatenate([(t[:, : 2 * GROUPS] * weight)[:, odd::2] for t in (c, -s)], axis=1)
        whole = twice(np.pad(np.tile(pick, (1, 3)), ((0, 0), (0, 4 * n - 6 * GROUPS))))
        z_inv.append(np.stack([whole[:, : 2 * n], whole[:, 2 * n :]]))
    return z_fwd, y_fwd, x_fwd, x_inv, y_inv, np.stack(z_inv).astype(np.float32)


def kernel(
    shift_ref, own_ref, other_ref, pad_own_ref, pad_other_ref, tab_ref,
    z_fwd_ref, y_fwd_ref, x_fwd_ref, x_inv_ref, y_inv_ref, z_inv_ref,
    out_ref,
    raw_ref, first_ref, pack_ref, high_ref, shifted_ref, spec_ref, freq_ref, cross_ref,
    wave_ref, line_ref, back_ref, forward_ref, xi_ref, yi_ref, zi_ref,
    *, bricks_y,
):
    n = BRICK
    w = 2 * n
    exp_index = lax.axis_index("exp")
    part = lax.axis_index("depth") // bricks_y
    columns = n + 2 * MARGIN
    pad = MARGIN * n
    strip = own_ref.shape[1]

    tab = tab_ref[...]
    rows = lax.broadcasted_iota(jnp.int32, (8, w), 0)
    offs = jnp.where(rows < 4, tab, pltpu.roll(tab, 4, 0))
    frac = jnp.where(rows < 4, pltpu.roll(tab, 4, 0), tab)
    total = sum(tent_value(float(d), frac) for d in range(-2, 4))
    parity = (rows >= 4).astype(f32)
    blocks = [tent_value(SHIFT_LOW + 2 * q + parity - offs, frac) / total for q in range(PAIRS)]
    sums = jnp.sum(sum(blocks)[:, :n], axis=1, keepdims=True) / n
    uniform = jnp.log(sums + pltpu.roll(jnp.broadcast_to(sums, (8, w)), 4, 0)[:, :1])
    both_high, back_low = [], []
    for block in blocks:
        high, low = split(block / 4.0)
        both_high += [high.astype(f32)] * 2
        back_low.append(low.astype(f32))
    stacked = jnp.concatenate(both_high + back_low + [jnp.zeros((40, w), f32)], axis=0)
    back_ref[...] = jnp.transpose(stacked)[:n, :224].astype(bf16)
    high, low = split(jnp.concatenate(blocks, axis=0) / n)
    forward_ref[...] = jnp.concatenate([high, low], axis=1)[:, : 3 * n]

    sz, sx, sy = (shift_ref[0, i] + n for i in range(3))
    moved = lax.rem(sx, n)
    turned = jnp.concatenate([x_inv_ref[0, pl.ds(moved, n), :], x_inv_ref[1, pl.ds(moved, n), :]], axis=0)
    high, low = split(turned)
    xi_ref[...] = jnp.concatenate([high, low], axis=1)[:, : 3 * n]
    lane = lax.broadcasted_iota(jnp.int32, (n, w), 1)
    back = lax.rem(w - lax.rem(sy, n), w)
    for ri_out in range(2):
        turned = pltpu.roll(y_inv_ref[ri_out], back, 1)
        pieces = []
        for ri in range(2):
            piece = turned[ri * n : (ri + 1) * n]
            pieces += [jnp.where(lane < n, piece, 0.0), jnp.where(lane < n, 0.0, piece)]
        high, low = split(jnp.concatenate(pieces, axis=0))
        at = slice(ri_out * w, (ri_out + 1) * w)
        yi_ref[0 : 2 * w, at] = high
        yi_ref[2 * w : 4 * w, at] = high
        yi_ref[4 * w :, at] = low
    first = lax.rem(HALF * exp_index + sz, n)
    turned = [jnp.concatenate([z_inv_ref[p, h, pl.ds(first, HALF), :] for h in range(2)], axis=1) for p in range(2)]
    turned = jnp.concatenate(turned, axis=0)
    high, low = split(turned)
    col = lax.broadcasted_iota(jnp.int32, turned.shape, 1)
    zi_ref[...] = jnp.where(col < 4 * GROUPS, high.astype(f32), low.astype(f32)).astype(bf16)[:, : 6 * GROUPS]

    def spread(first_lane, count):
        pieces = [pack_ref[:, pl.ds(first_lane + 2 * w * q, count)] for q in range(PAIRS)]
        pieces += [high_ref[:, pl.ds(first_lane + 2 * w * q, count)] for q in range(0, PAIRS, 2)]
        return jnp.concatenate(pieces, axis=0)

    def pack(both):
        lanes = both.shape[1]
        high = both.astype(bf16).astype(f32)
        pack_ref[:, 0:lanes] = jnp.concatenate([high, both - high], axis=0).astype(bf16)
        later = jnp.concatenate([high[:, 2 * w :], high[:, : 2 * w]], axis=1)
        high_ref[:, 0:lanes] = jnp.concatenate([high, later], axis=0).astype(bf16)

    raw_ref[0:4, 0:pad] = pad_own_ref[0]
    raw_ref[4:8, 0:pad] = pad_other_ref[0]
    raw_ref[0:4, pad : pad + strip] = own_ref[...]
    raw_ref[4:8, pad : pad + strip] = other_ref[...]
    raw_ref[0:4, pad + strip :] = pad_own_ref[pad_own_ref.shape[0] - 1]
    raw_ref[4:8, pad + strip :] = pad_other_ref[pad_other_ref.shape[0] - 1]
    row = lax.broadcasted_iota(jnp.int32, (8, w), 0)
    lane = lax.broadcasted_iota(jnp.int32, (8, w), 1)
    same = (row < 4) == (lane < n)
    swap = lambda v: pltpu.roll(v, n, 1)
    ratio = jnp.log(raw_ref[:, pl.ds(pl.multiple_of(part * (n * n), n * n), columns * n)]) - uniform
    even, odd = [], []
    for k in range(columns // 2):
        here = ratio[:, k * w : (k + 1) * w]
        flipped = pltpu.roll(here, 4, 0)
        even.append(jnp.where(same, here, swap(flipped)))
        odd.append(jnp.where(same, swap(here), flipped))
    cols = []
    for k in range(columns // 2):
        cols += [even[k], jnp.where(row < 4, odd[k], odd[(k + 1) % (columns // 2)])]
    cols = jnp.concatenate(cols, axis=1)
    first_ref[...] = cols
    pack(cols)

    lo_x, hi_x = -REACH, n + REACH
    chunk = 20 * w
    back_w = back_ref[...]
    forward_w = forward_ref[...]

    def first_pass(i, _):
        start = pl.multiple_of(i * chunk, 2 * w)
        logv = dot(back_w, spread(start + (lo_x + SHIFT_LOW + MARGIN) * w, chunk))
        high, low = split(jnp.exp(logv))
        shifted_ref[:, pl.ds(start, chunk)] = dot(forward_w, jnp.concatenate([high, low, high], axis=0))
        return 0

    lax.fori_loop(0, (hi_x - lo_x) * w // chunk, first_pass, 0)

    lo_u, hi_u = -10, n + 10
    count = (hi_u - lo_u) * w
    gathered = sum(
        shifted_ref[8 * q : 8 * q + 8, pl.ds((lo_u - SHIFT_LOW - 2 * q - lo_x) * w, count)] for q in range(PAIRS)
    )
    proj = gathered[:, 2 * w :] + pltpu.roll(gathered[:, w : count - w], 4, 0)
    ratio = first_ref[:, (lo_u + 2 + MARGIN) * w : (hi_u + MARGIN) * w]
    ratio = ratio + (ratio + uniform - jnp.log(proj))
    later = pltpu.roll(jnp.concatenate([ratio[:, w:], ratio[:, :w]], axis=1), 4, 0)
    pack(jnp.where(lax.broadcasted_iota(jnp.int32, ratio.shape, 0) < 4, ratio, later))

    per = 16
    chunk2 = per * w

    def second_pass(i, _):
        start = pl.multiple_of(i * chunk2, chunk2)
        logv = dot(back_w, spread(start, chunk2))
        high, low = split(jnp.exp(logv))
        spec = dot(z_fwd_ref[...], jnp.concatenate([high, low, high], axis=0))
        groups = []
        for j in range(per):
            piece = spec[:, w * j : w * (j + 1)]
            groups.append(jnp.concatenate([piece[:ROWS], piece[ROWS:]], axis=1))
        high, low = split(jnp.concatenate(groups, axis=0))
        lines = dot(jnp.concatenate([high, low, high], axis=1), y_fwd_ref[...])
        at = pl.multiple_of(i * (per * ROWS), per * ROWS)
        spec_ref[0, pl.ds(at, per * ROWS), :] = lines[:, :w]
        spec_ref[1, pl.ds(at, per * ROWS), :] = lines[:, w:]
        return 0

    lax.fori_loop(0, n // per, second_pass, 0)

    lane = lax.broadcasted_iota(jnp.int32, (n, w), 1)
    row = lax.broadcasted_iota(jnp.int32, (n, w), 0)
    own_sign = jnp.where(exp_index == 0, 1.0, -1.0)
    exp_sign = jnp.where(lane < n, own_sign, -own_sign)
    anchor = (lane == 0) & (row == 0)

    def three(value):
        high, low = split(value)
        return jnp.concatenate([high, low, high], axis=0)

    def spectra(i, _):
        for t in range(UNROLL):
            at = jnp.maximum(i - 2, 0) * UNROLL + t
            both = dot(xi_ref[...], cross_ref[t])
            re = both[:n, :w] - both[n:, w:]
            im = both[:n, w:] + both[n:, :w]
            high, low = split(jnp.concatenate([re, im], axis=1))
            wave_ref[0, pl.ds(pl.multiple_of(at * n, n), n), :] = high
            wave_ref[1, pl.ds(pl.multiple_of(at * n, n), n), :] = low
        for t in range(UNROLL):
            re_a, im_a = freq_ref[t, 0, 0], freq_ref[t, 0, 1]
            re_b, im_b = freq_ref[t, 1, 0], freq_ref[t, 1, 1]
            re_one = jnp.where(lane < n, re_a, re_b)
            im_one = jnp.where(lane < n, im_a, im_b)
            re_two = swap(jnp.where(lane < n, re_b, re_a))
            im_two = swap(jnp.where(lane < n, im_b, im_a))
            power = (re_one * re_one + im_one * im_one) * (re_two * re_two + im_two * im_two)
            gain = lax.rsqrt(jnp.maximum(power, spectral_floor * spectral_floor))
            if t == 0:
                gain = jnp.where(anchor & (i == 1), 0.0, gain)
            cross_re = (re_one * re_two + im_one * im_two) * gain
            cross_im = (re_one * im_two - im_one * re_two) * (gain * exp_sign)
            cross_ref[t] = three(jnp.concatenate([cross_re, cross_im], axis=1))
        for t in range(UNROLL):
            for odd in range(2):
                kz = jnp.minimum(i, STEPS - 1) * (2 * UNROLL) + 2 * t + odd
                lines = [spec_ref[ri, pl.ds(kz, n, stride=ROWS), :] for ri in range(2)]
                both = dot(x_fwd_ref[...], three(jnp.concatenate(lines, axis=1)))
                freq_ref[t, odd, 0] = both[:n, :w] + both[n:, w:]
                freq_ref[t, odd, 1] = both[:n, w:] - both[n:, :w]
        return 0

    lax.fori_loop(0, STEPS + 2, spectra, 0)

    done = STEPS * UNROLL
    per = done // 2

    def inverse_y(i, _):
        at = pl.multiple_of(i * (per * n), per * n)
        high, low = wave_ref[0, pl.ds(at, per * n), :], wave_ref[1, pl.ds(at, per * n), :]
        lines = dot(jnp.concatenate([high, low, high], axis=1), yi_ref[...])
        for t in range(per):
            to = pl.multiple_of((i * per + t) * GAP, 8)
            line_ref[0, pl.ds(to, n), :] = lines[t * n : (t + 1) * n, :w]
            line_ref[1, pl.ds(to, n), :] = lines[t * n : (t + 1) * n, w:]
        return 0

    lax.fori_loop(0, 2, inverse_y, 0)
    line_ref[:, done * GAP :, :] = jnp.zeros((2, (GROUPS - done) * GAP, w), f32)

    lane = lax.broadcasted_iota(jnp.int32, (HALF, w), 1)
    x_per_step = 8

    def planes(i, _):
        for t in range(x_per_step):
            pair = i * x_per_step + t
            cols = jnp.concatenate(
                [
                    jnp.concatenate([line_ref[ri, pl.ds(2 * pair + p, GROUPS, stride=GAP), :] for ri in range(2)], axis=0)
                    for p in range(2)
                ],
                axis=1,
            )
            both = dot(zi_ref[...], three(cols))
            a_even, a_odd = both[:HALF, :w], both[:HALF, w:]
            b_even, b_odd = both[HALF:, :w], both[HALF:, w:]
            value = jnp.where(lane < n, a_even, b_odd) + swap(jnp.where(lane < n, a_odd, b_even))
            out_ref[:, pl.ds(pl.multiple_of(pair * w, w), w)] = value
        return 0

    lax.fori_loop(0, HALF // x_per_step, planes, 0)


def share_tables(offsets, fractions):
    both = jnp.concatenate([offsets.astype(f32), fractions], axis=0)
    count = lax.axis_size("depth")
    slab = both.shape[1]
    lane = jnp.arange(2 * count * slab, dtype=jnp.int32) % (count * slab)
    mine = (lane // slab == lax.axis_index("depth")).astype(f32)
    table = jnp.tile(both, (1, 2 * count)) * mine
    step = 1
    while step < count:
        table = table + lax.ppermute(table, "depth", [(i, i ^ step) for i in range(count)])
        step *= 2
    return table


def windows(images, bricks_x, bricks_y):
    exps, tiles, depths = (lax.axis_size(a) for a in ("exp", "tile", "depth"))
    depth_index = lax.axis_index("depth")
    cams = images.shape[1]
    strip = lax.dynamic_slice_in_dim(images[0], depth_index % bricks_y * BRICK, BRICK, axis=2).reshape(cams, -1)

    def linear(e, t, d):
        return ((e % exps) * tiles + t % tiles) * depths + d

    def edge(step, other):
        edge_part = 0 if step == 1 else bricks_x - 1
        return [
            (linear(e, t, d), linear(e + other, t + step, d))
            for e in range(exps)
            for t in range(tiles)
            for d in range(depths)
            if d // bricks_y == edge_part
        ]

    axes = ("exp", "tile", "depth")
    tail = strip[:, -MARGIN * BRICK :]
    head = strip[:, : MARGIN * BRICK]
    pads = []
    for other in (0, 1):
        if bricks_x > 1:
            sent = jnp.where(depth_index // bricks_y == 0, tail, head)
            pads.append(lax.ppermute(sent, axes, edge(1, other) + edge(-1, other))[None])
        else:
            pads.append(jnp.stack([lax.ppermute(tail, axes, edge(1, other)), lax.ppermute(head, axes, edge(-1, other))]))
    other_strip = lax.ppermute(strip, "exp", [(i, (i + 1) % exps) for i in range(exps)])
    return strip, other_strip, pads[0], pads[1]


def per_device(images, offsets, fractions, shifts):
    cams, width, rows_y = images.shape[1:]
    bricks_x, bricks_y = width // BRICK, rows_y // BRICK
    assert cams == 4 and width % BRICK == 0 and rows_y % BRICK == 0
    assert bricks_x * bricks_y == lax.axis_size("depth")
    assert offsets.shape[1] * lax.axis_size("depth") == BRICK
    n = BRICK
    table = share_tables(offsets, fractions)
    strips = windows(images, bricks_x, bricks_y)
    window = (n + 2 * MARGIN) * n
    extended = (width + 2 * MARGIN) * n
    vmem = pl.BlockSpec(memory_space=pltpu.VMEM)
    out = pl.pallas_call(
        functools.partial(kernel, bricks_y=bricks_y),
        out_shape=jax.ShapeDtypeStruct((HALF, n * n), f32),
        in_specs=[pl.BlockSpec(memory_space=pltpu.SMEM)] + [vmem] * 11,
        out_specs=vmem,
        scratch_shapes=[
            pltpu.VMEM((8, extended), f32),
            pltpu.VMEM((8, 2 * window), f32),
            pltpu.VMEM((16, 2 * window), bf16),
            pltpu.VMEM((16, 2 * window), bf16),
            pltpu.VMEM((8 * PAIRS, (n + 2 * REACH) * 2 * n), f32),
            pltpu.VMEM((2, n * ROWS, 2 * n), f32),
            pltpu.VMEM((UNROLL, 2, 2, n, 2 * n), f32),
            pltpu.VMEM((UNROLL, 3 * n, 4 * n), bf16),
            pltpu.VMEM((2, STEPS * UNROLL * n, 4 * n), bf16),
            pltpu.VMEM((2, GROUPS * GAP, 2 * n), f32),
            pltpu.VMEM((n, 224), bf16),
            pltpu.VMEM((8 * PAIRS, 3 * n), bf16),
            pltpu.VMEM((2 * n, 3 * n), bf16),
            pltpu.VMEM((12 * n, 4 * n), bf16),
            pltpu.VMEM((n, 6 * GROUPS), bf16),
        ],
        compiler_params=pltpu.CompilerParams(vmem_limit_bytes=40 * 1024 * 1024),
    )(shifts, *strips, table, *(jnp.asarray(t) for t in constant_tables()))
    return out.reshape(1, HALF, n * n)


def solution(mesh):
    placed = (
        P("exp", None, "tile", None),
        P(None, "depth"),
        P(None, "depth"),
        P(("tile", "depth"), None),
    )
    return jax.shard_map(
        per_device,
        mesh=mesh,
        in_specs=placed,
        out_specs=P(("tile", "depth"), "exp", None),
        check_vma=False,
    )
```

```python
import functools
import math

import jax
import jax.numpy as jnp
import numpy as np
from jax import lax
from jax.experimental import pallas as pl
from jax.experimental.pallas import tpu as pltpu
from jax.sharding import PartitionSpec as P


BRICK = 64
HALF = BRICK // 2
ROWS = 40
MARGIN = 32
SHIFT_LOW = -8
PAIRS = 9
REACH = 18
UNROLL = 2
STEPS = 9
GROUPS = 24
GAP = 72
spectral_floor = 0.01
f32, bf16 = jnp.float32, jnp.bfloat16


def split(value):
    high = value.astype(bf16)
    return high, (value - high.astype(f32)).astype(bf16)


def dot(a, b):
    return jnp.dot(a, b, preferred_element_type=f32)


def tent_value(distance, fraction):
    return jnp.maximum(0.0, 1.0 - jnp.abs(distance - fraction) / 1.5)


def dft_parts():
    wave = np.arange(BRICK)
    angle = (wave[:, None] * wave[None, :] % BRICK) * (2.0 * math.pi / BRICK)
    return np.cos(angle) / math.sqrt(BRICK), np.sin(angle) / math.sqrt(BRICK)


def host_split(value):
    high = value.astype(np.float32).astype(bf16)
    return high, (value - high.astype(np.float64)).astype(np.float32).astype(bf16)


def constant_tables():
    c, s = dft_parts()
    n = BRICK
    zt = np.zeros((2 * ROWS, n))
    zt[: HALF + 1], zt[ROWS : ROWS + HALF + 1] = c[: HALF + 1], -s[: HALF + 1]
    high, low = host_split(zt)
    z_fwd = np.concatenate([high, high, low], axis=1)
    yt = np.zeros((2, 2, n, 2, 2, n))
    for e in range(2):
        yt[0, e, :, 0, e], yt[0, e, :, 1, e] = c, -s
        yt[1, e, :, 0, e], yt[1, e, :, 1, e] = s, c
    high, low = host_split(yt.reshape(4 * n, 4 * n))
    y_fwd = np.concatenate([high, high, low], axis=0)
    high, low = host_split(np.concatenate([c, s], axis=0))
    x_fwd = np.concatenate([high, high, low], axis=1)
    twice = lambda t: np.concatenate([t, t], axis=0)
    x_inv = np.stack([np.tile(twice(t), (1, 2)) for t in (c, s)]).astype(np.float32)
    y_inv = np.stack([np.concatenate([twice(c), twice(-s)], 1).T, np.concatenate([twice(s), twice(c)], 1).T])
    y_inv = y_inv.astype(np.float32)
    weight = np.zeros(2 * GROUPS)
    weight[: HALF + 1] = 2.0
    weight[0] = weight[HALF] = 1.0
    z_inv = []
    for odd in range(2):
        pick = np.concatenate([(t[:, : 2 * GROUPS] * weight)[:, odd::2] for t in (c, -s)], axis=1)
        whole = twice(np.pad(np.tile(pick, (1, 3)), ((0, 0), (0, 4 * n - 6 * GROUPS))))
        z_inv.append(np.stack([whole[:, : 2 * n], whole[:, 2 * n :]]))
    return z_fwd, y_fwd, x_fwd, x_inv, y_inv, np.stack(z_inv).astype(np.float32)


def kernel(
    shift_hbm, own_ref, other_ref, pad_own_ref, pad_other_ref, tab_ref,
    z_fwd_ref, y_fwd_ref, x_fwd_ref, x_inv_ref, y_inv_ref, z_inv_ref,
    out_hbm,
    raw_ref, first_ref, pack_ref, high_ref, shifted_ref, spec_ref, freq_ref, cross_ref,
    wave_ref, line_ref, back_ref, forward_ref, xi_ref, yi_ref, zi_ref,
    out_ref, shift_ref, shift_sem, out_sem,
    *, bricks_y,
):
    n = BRICK
    w = 2 * n
    exp_index = lax.axis_index("exp")
    part = lax.axis_index("depth") // bricks_y
    columns = n + 2 * MARGIN
    pad = MARGIN * n
    strip = own_ref.shape[1]
    shift_copy = pltpu.make_async_copy(shift_hbm, shift_ref, shift_sem)
    shift_copy.start()

    tab = tab_ref[...]
    rows = lax.broadcasted_iota(jnp.int32, (8, w), 0)
    offs = jnp.where(rows < 4, tab, pltpu.roll(tab, 4, 0))
    frac = jnp.where(rows < 4, pltpu.roll(tab, 4, 0), tab)
    total = sum(tent_value(float(d), frac) for d in range(-2, 4))
    parity = (rows >= 4).astype(f32)
    blocks = [tent_value(SHIFT_LOW + 2 * q + parity - offs, frac) / total for q in range(PAIRS)]
    sums = jnp.sum(sum(blocks)[:, :n], axis=1, keepdims=True) / n
    uniform = jnp.log(sums + pltpu.roll(jnp.broadcast_to(sums, (8, w)), 4, 0)[:, :1])
    both_high, back_low = [], []
    for block in blocks:
        high, low = split(block / 4.0)
        both_high += [high.astype(f32)] * 2
        back_low.append(low.astype(f32))
    stacked = jnp.concatenate(both_high + back_low + [jnp.zeros((40, w), f32)], axis=0)
    back_ref[...] = jnp.transpose(stacked)[:n, :224].astype(bf16)
    high, low = split(jnp.concatenate(blocks, axis=0) / n)
    forward_ref[...] = jnp.concatenate([high, low], axis=1)[:, : 3 * n]

    def spread(first_lane, count):
        pieces = [pack_ref[:, pl.ds(first_lane + 2 * w * q, count)] for q in range(PAIRS)]
        pieces += [high_ref[:, pl.ds(first_lane + 2 * w * q, count)] for q in range(0, PAIRS, 2)]
        return jnp.concatenate(pieces, axis=0)

    def pack(both):
        lanes = both.shape[1]
        high = both.astype(bf16).astype(f32)
        pack_ref[:, 0:lanes] = jnp.concatenate([high, both - high], axis=0).astype(bf16)
        later = jnp.concatenate([high[:, 2 * w :], high[:, : 2 * w]], axis=1)
        high_ref[:, 0:lanes] = jnp.concatenate([high, later], axis=0).astype(bf16)

    raw_ref[0:4, 0:pad] = pad_own_ref[0]
    raw_ref[4:8, 0:pad] = pad_other_ref[0]
    raw_ref[0:4, pad : pad + strip] = own_ref[...]
    raw_ref[4:8, pad : pad + strip] = other_ref[...]
    raw_ref[0:4, pad + strip :] = pad_own_ref[pad_own_ref.shape[0] - 1]
    raw_ref[4:8, pad + strip :] = pad_other_ref[pad_other_ref.shape[0] - 1]
    row = lax.broadcasted_iota(jnp.int32, (8, w), 0)
    lane = lax.broadcasted_iota(jnp.int32, (8, w), 1)
    same = (row < 4) == (lane < n)
    swap = lambda v: pltpu.roll(v, n, 1)
    ratio = jnp.log(raw_ref[:, pl.ds(pl.multiple_of(part * (n * n), n * n), columns * n)]) - uniform
    even, odd = [], []
    for k in range(columns // 2):
        here = ratio[:, k * w : (k + 1) * w]
        flipped = pltpu.roll(here, 4, 0)
        even.append(jnp.where(same, here, swap(flipped)))
        odd.append(jnp.where(same, swap(here), flipped))
    cols = []
    for k in range(columns // 2):
        cols += [even[k], jnp.where(row < 4, odd[k], odd[(k + 1) % (columns // 2)])]
    cols = jnp.concatenate(cols, axis=1)
    first_ref[...] = cols
    pack(cols)

    lo_x, hi_x = -REACH, n + REACH
    chunk = 20 * w
    back_w = back_ref[...]
    forward_w = forward_ref[...]

    def first_pass(i, _):
        start = pl.multiple_of(i * chunk, 2 * w)
        logv = dot(back_w, spread(start + (lo_x + SHIFT_LOW + MARGIN) * w, chunk))
        high, low = split(jnp.exp(logv))
        shifted_ref[:, pl.ds(start, chunk)] = dot(forward_w, jnp.concatenate([high, low, high], axis=0))
        return 0

    lax.fori_loop(0, (hi_x - lo_x) * w // chunk, first_pass, 0)

    lo_u, hi_u = -10, n + 10
    count = (hi_u - lo_u) * w
    gathered = sum(
        shifted_ref[8 * q : 8 * q + 8, pl.ds((lo_u - SHIFT_LOW - 2 * q - lo_x) * w, count)] for q in range(PAIRS)
    )
    proj = gathered[:, 2 * w :] + pltpu.roll(gathered[:, w : count - w], 4, 0)
    ratio = first_ref[:, (lo_u + 2 + MARGIN) * w : (hi_u + MARGIN) * w]
    ratio = ratio + (ratio + uniform - jnp.log(proj))
    later = pltpu.roll(jnp.concatenate([ratio[:, w:], ratio[:, :w]], axis=1), 4, 0)
    pack(jnp.where(lax.broadcasted_iota(jnp.int32, ratio.shape, 0) < 4, ratio, later))

    shift_copy.wait()
    sz, sx, sy = (shift_ref[0, i] + n for i in range(3))
    moved = lax.rem(sx, n)
    turned = jnp.concatenate([x_inv_ref[0, pl.ds(moved, n), :], x_inv_ref[1, pl.ds(moved, n), :]], axis=0)
    high, low = split(turned)
    xi_ref[...] = jnp.concatenate([high, low], axis=1)[:, : 3 * n]
    lane = lax.broadcasted_iota(jnp.int32, (n, w), 1)
    back = lax.rem(w - lax.rem(sy, n), w)
    for ri_out in range(2):
        turned = pltpu.roll(y_inv_ref[ri_out], back, 1)
        pieces = []
        for ri in range(2):
            piece = turned[ri * n : (ri + 1) * n]
            pieces += [jnp.where(lane < n, piece, 0.0), jnp.where(lane < n, 0.0, piece)]
        high, low = split(jnp.concatenate(pieces, axis=0))
        at = slice(ri_out * w, (ri_out + 1) * w)
        yi_ref[0 : 2 * w, at] = high
        yi_ref[2 * w : 4 * w, at] = high
        yi_ref[4 * w :, at] = low
    first = lax.rem(HALF * exp_index + sz, n)
    turned = [jnp.concatenate([z_inv_ref[p, h, pl.ds(first, HALF), :] for h in range(2)], axis=1) for p in range(2)]
    turned = jnp.concatenate(turned, axis=0)
    high, low = split(turned)
    col = lax.broadcasted_iota(jnp.int32, turned.shape, 1)
    zi_ref[...] = jnp.where(col < 4 * GROUPS, high.astype(f32), low.astype(f32)).astype(bf16)[:, : 6 * GROUPS]

    per = 16
    chunk2 = per * w

    def second_pass(i, _):
        start = pl.multiple_of(i * chunk2, chunk2)
        logv = dot(back_w, spread(start, chunk2))
        high, low = split(jnp.exp(logv))
        spec = dot(z_fwd_ref[...], jnp.concatenate([high, low, high], axis=0))
        groups = []
        for j in range(per):
            piece = spec[:, w * j : w * (j + 1)]
            groups.append(jnp.concatenate([piece[:ROWS], piece[ROWS:]], axis=1))
        high, low = split(jnp.concatenate(groups, axis=0))
        lines = dot(jnp.concatenate([high, low, high], axis=1), y_fwd_ref[...])
        at = pl.multiple_of(i * (per * ROWS), per * ROWS)
        spec_ref[0, pl.ds(at, per * ROWS), :] = lines[:, :w]
        spec_ref[1, pl.ds(at, per * ROWS), :] = lines[:, w:]
        return 0

    lax.fori_loop(0, n // per, second_pass, 0)

    lane = lax.broadcasted_iota(jnp.int32, (n, w), 1)
    row = lax.broadcasted_iota(jnp.int32, (n, w), 0)
    own_sign = jnp.where(exp_index == 0, 1.0, -1.0)
    exp_sign = jnp.where(lane < n, own_sign, -own_sign)
    anchor = (lane == 0) & (row == 0)

    def three(value):
        high, low = split(value)
        return jnp.concatenate([high, low, high], axis=0)

    def spectra(i, _):
        for t in range(UNROLL):
            at = jnp.maximum(i - 2, 0) * UNROLL + t
            both = dot(xi_ref[...], cross_ref[t])
            re = both[:n, :w] - both[n:, w:]
            im = both[:n, w:] + both[n:, :w]
            high, low = split(jnp.concatenate([re, im], axis=1))
            wave_ref[0, pl.ds(pl.multiple_of(at * n, n), n), :] = high
            wave_ref[1, pl.ds(pl.multiple_of(at * n, n), n), :] = low
        for t in range(UNROLL):
            re_a, im_a = freq_ref[t, 0, 0], freq_ref[t, 0, 1]
            re_b, im_b = freq_ref[t, 1, 0], freq_ref[t, 1, 1]
            re_one = jnp.where(lane < n, re_a, re_b)
            im_one = jnp.where(lane < n, im_a, im_b)
            re_two = swap(jnp.where(lane < n, re_b, re_a))
            im_two = swap(jnp.where(lane < n, im_b, im_a))
            power = (re_one * re_one + im_one * im_one) * (re_two * re_two + im_two * im_two)
            gain = lax.rsqrt(jnp.maximum(power, spectral_floor * spectral_floor))
            if t == 0:
                gain = jnp.where(anchor & (i == 1), 0.0, gain)
            cross_re = (re_one * re_two + im_one * im_two) * gain
            cross_im = (re_one * im_two - im_one * re_two) * (gain * exp_sign)
            cross_ref[t] = three(jnp.concatenate([cross_re, cross_im], axis=1))
        for t in range(UNROLL):
            for odd in range(2):
                kz = jnp.minimum(i, STEPS - 1) * (2 * UNROLL) + 2 * t + odd
                lines = [spec_ref[ri, pl.ds(kz, n, stride=ROWS), :] for ri in range(2)]
                both = dot(x_fwd_ref[...], three(jnp.concatenate(lines, axis=1)))
                freq_ref[t, odd, 0] = both[:n, :w] + both[n:, w:]
                freq_ref[t, odd, 1] = both[:n, w:] - both[n:, :w]
        return 0

    lax.fori_loop(0, STEPS + 2, spectra, 0)

    done = STEPS * UNROLL
    per = done // 2

    def inverse_y(i, _):
        at = pl.multiple_of(i * (per * n), per * n)
        high, low = wave_ref[0, pl.ds(at, per * n), :], wave_ref[1, pl.ds(at, per * n), :]
        lines = dot(jnp.concatenate([high, low, high], axis=1), yi_ref[...])
        for t in range(per):
            to = pl.multiple_of((i * per + t) * GAP, 8)
            line_ref[0, pl.ds(to, n), :] = lines[t * n : (t + 1) * n, :w]
            line_ref[1, pl.ds(to, n), :] = lines[t * n : (t + 1) * n, w:]
        return 0

    lax.fori_loop(0, 2, inverse_y, 0)
    line_ref[:, done * GAP :, :] = jnp.zeros((2, (GROUPS - done) * GAP, w), f32)

    lane = lax.broadcasted_iota(jnp.int32, (HALF, w), 1)
    x_per_step = 8

    def planes(i, _):
        for t in range(x_per_step):
            pair = i * x_per_step + t
            cols = jnp.concatenate(
                [
                    jnp.concatenate([line_ref[ri, pl.ds(2 * pair + p, GROUPS, stride=GAP), :] for ri in range(2)], axis=0)
                    for p in range(2)
                ],
                axis=1,
            )
            both = dot(zi_ref[...], three(cols))
            a_even, a_odd = both[:HALF, :w], both[:HALF, w:]
            b_even, b_odd = both[HALF:, :w], both[HALF:, w:]
            value = jnp.where(lane < n, a_even, b_odd) + swap(jnp.where(lane < n, a_odd, b_even))
            out_ref[:, pl.ds(pl.multiple_of(pair * w, w), w)] = value
        out_copy(i).start()
        return 0

    def out_copy(i):
        at = pl.ds(pl.multiple_of(i * (x_per_step * w), x_per_step * w), x_per_step * w)
        return pltpu.make_async_copy(out_ref.at[:, at], out_hbm.at[:, at], out_sem.at[i])

    lax.fori_loop(0, HALF // x_per_step, planes, 0)
    for i in range(HALF // x_per_step):
        out_copy(i).wait()


def share_tables(offsets, fractions):
    both = jnp.concatenate([offsets.astype(f32), fractions], axis=0)
    count = lax.axis_size("depth")
    slab = both.shape[1]
    lane = jnp.arange(2 * count * slab, dtype=jnp.int32) % (count * slab)
    mine = (lane // slab == lax.axis_index("depth")).astype(f32)
    table = jnp.tile(both, (1, 2 * count)) * mine
    step = count // 2
    while step > 2:
        table = table + lax.ppermute(table, "depth", [(i, i ^ step) for i in range(count)])
        step //= 2
    total = table
    for k in (1, 2, 3):
        total = total + lax.ppermute(table, "depth", [(i, i ^ k) for i in range(count)])
    return total


def windows(images, bricks_x, bricks_y):
    exps, tiles, depths = (lax.axis_size(a) for a in ("exp", "tile", "depth"))
    depth_index = lax.axis_index("depth")
    cams = images.shape[1]
    strip = lax.dynamic_slice_in_dim(images[0], depth_index % bricks_y * BRICK, BRICK, axis=2).reshape(cams, -1)

    def linear(e, t, d):
        return ((e % exps) * tiles + t % tiles) * depths + d

    def edge(step, other):
        edge_part = 0 if step == 1 else bricks_x - 1
        return [
            (linear(e, t, d), linear(e + other, t + step, d))
            for e in range(exps)
            for t in range(tiles)
            for d in range(depths)
            if d // bricks_y == edge_part
        ]

    axes = ("exp", "tile", "depth")
    tail = strip[:, -MARGIN * BRICK :]
    head = strip[:, : MARGIN * BRICK]
    pads = []
    for other in (0, 1):
        if bricks_x > 1:
            sent = jnp.where(depth_index // bricks_y == 0, tail, head)
            pads.append(lax.ppermute(sent, axes, edge(1, other) + edge(-1, other))[None])
        else:
            sides = ((tail, 1), (head, -1))
            pads.append(jnp.stack([lax.ppermute(v, axes, edge(step, other)) for v, step in sides]))
    other_strip = lax.ppermute(strip, "exp", [(i, (i + 1) % exps) for i in range(exps)])
    return strip, other_strip, pads[0], pads[1]


def per_device(images, offsets, fractions, shifts):
    cams, width, rows_y = images.shape[1:]
    bricks_x, bricks_y = width // BRICK, rows_y // BRICK
    assert cams == 4 and width % BRICK == 0 and rows_y % BRICK == 0
    assert bricks_x * bricks_y == lax.axis_size("depth")
    assert offsets.shape[1] * lax.axis_size("depth") == BRICK
    n = BRICK
    table = share_tables(offsets, fractions)
    strips = windows(images, bricks_x, bricks_y)
    window = (n + 2 * MARGIN) * n
    extended = (width + 2 * MARGIN) * n
    vmem = pl.BlockSpec(memory_space=pltpu.VMEM)
    out = pl.pallas_call(
        functools.partial(kernel, bricks_y=bricks_y),
        out_shape=jax.ShapeDtypeStruct((HALF, n * n), f32),
        in_specs=[pl.BlockSpec(memory_space=pltpu.HBM)] + [vmem] * 11,
        out_specs=pl.BlockSpec(memory_space=pl.ANY),
        scratch_shapes=[
            pltpu.VMEM((8, extended), f32),
            pltpu.VMEM((8, 2 * window), f32),
            pltpu.VMEM((16, 2 * window), bf16),
            pltpu.VMEM((16, 2 * window), bf16),
            pltpu.VMEM((8 * PAIRS, (n + 2 * REACH) * 2 * n), f32),
            pltpu.VMEM((2, n * ROWS, 2 * n), f32),
            pltpu.VMEM((UNROLL, 2, 2, n, 2 * n), f32),
            pltpu.VMEM((UNROLL, 3 * n, 4 * n), bf16),
            pltpu.VMEM((2, STEPS * UNROLL * n, 4 * n), bf16),
            pltpu.VMEM((2, GROUPS * GAP, 2 * n), f32),
            pltpu.VMEM((n, 224), bf16),
            pltpu.VMEM((8 * PAIRS, 3 * n), bf16),
            pltpu.VMEM((2 * n, 3 * n), bf16),
            pltpu.VMEM((12 * n, 4 * n), bf16),
            pltpu.VMEM((n, 6 * GROUPS), bf16),
            pltpu.VMEM((HALF, n * n), f32),
            pltpu.SMEM(shifts.shape, jnp.int32),
            pltpu.SemaphoreType.DMA(()),
            pltpu.SemaphoreType.DMA((4,)),
        ],
        compiler_params=pltpu.CompilerParams(vmem_limit_bytes=40 * 1024 * 1024),
    )(shifts, *strips, table, *(jnp.asarray(t) for t in constant_tables()))
    return out.reshape(1, HALF, n * n)


def solution(mesh):
    placed = (
        P("exp", None, "tile", None),
        P(None, "depth"),
        P(None, "depth"),
        P(("tile", "depth"), None),
    )
    return jax.shard_map(
        per_device,
        mesh=mesh,
        in_specs=placed,
        out_specs=P(("tile", "depth"), "exp", None),
        check_vma=False,
    )
```

```python
import functools
import math

import jax
import jax.numpy as jnp
import numpy as np
from jax import lax
from jax.experimental import pallas as pl
from jax.experimental.pallas import tpu as pltpu
from jax.sharding import PartitionSpec as P


BRICK = 64
HALF = BRICK // 2
ROWS = 40
MARGIN = 32
SHIFT_LOW = -8
PAIRS = 9
REACH = 18
UNROLL = 2
STEPS = 9
GROUPS = 24
GAP = 72
spectral_floor = 0.01
f32, bf16 = jnp.float32, jnp.bfloat16


def split(value):
    high = value.astype(bf16)
    return high, (value - high.astype(f32)).astype(bf16)


def dot(a, b):
    return jnp.dot(a, b, preferred_element_type=f32)


def tent_value(distance, fraction):
    return jnp.maximum(0.0, 1.0 - jnp.abs(distance - fraction) / 1.5)


def dft_parts():
    wave = np.arange(BRICK)
    angle = (wave[:, None] * wave[None, :] % BRICK) * (2.0 * math.pi / BRICK)
    return np.cos(angle) / math.sqrt(BRICK), np.sin(angle) / math.sqrt(BRICK)


def host_split(value):
    high = value.astype(np.float32).astype(bf16)
    return high, (value - high.astype(np.float64)).astype(np.float32).astype(bf16)


def constant_tables():
    c, s = dft_parts()
    n = BRICK
    zt = np.zeros((2 * ROWS, n))
    zt[: HALF + 1], zt[ROWS : ROWS + HALF + 1] = c[: HALF + 1], -s[: HALF + 1]
    high, low = host_split(zt)
    z_fwd = np.concatenate([high, high, low], axis=1)
    yt = np.zeros((2, 2, n, 2, 2, n))
    for e in range(2):
        yt[0, e, :, 0, e], yt[0, e, :, 1, e] = c, -s
        yt[1, e, :, 0, e], yt[1, e, :, 1, e] = s, c
    high, low = host_split(yt.reshape(4 * n, 4 * n))
    y_fwd = np.concatenate([high, high, low], axis=0)
    high, low = host_split(np.concatenate([c, s], axis=0))
    x_fwd = np.concatenate([high, high, low], axis=1)
    twice = lambda t: np.concatenate([t, t], axis=0)
    x_inv = np.stack([np.tile(twice(t), (1, 2)) for t in (c, s)]).astype(np.float32)
    y_inv = np.stack([np.concatenate([twice(c), twice(-s)], 1).T, np.concatenate([twice(s), twice(c)], 1).T])
    y_inv = y_inv.astype(np.float32)
    weight = np.zeros(2 * GROUPS)
    weight[: HALF + 1] = 2.0
    weight[0] = weight[HALF] = 1.0
    z_inv = []
    for odd in range(2):
        pick = np.concatenate([(t[:, : 2 * GROUPS] * weight)[:, odd::2] for t in (c, -s)], axis=1)
        whole = twice(np.pad(np.tile(pick, (1, 3)), ((0, 0), (0, 4 * n - 6 * GROUPS))))
        z_inv.append(np.stack([whole[:, : 2 * n], whole[:, 2 * n :]]))
    return z_fwd, y_fwd, x_fwd, x_inv, y_inv, np.stack(z_inv).astype(np.float32)


def pack(both, pack_ref, high_ref):
    w = 2 * BRICK
    high = both.astype(bf16).astype(f32)
    pack_ref[...] = jnp.concatenate([high, both - high], axis=0).astype(bf16)
    later = jnp.concatenate([high[:, 2 * w :], high[:, : 2 * w]], axis=1)
    high_ref[...] = jnp.concatenate([high, later], axis=0).astype(bf16)


def turn(shift_ref, x_inv_ref, y_inv_ref, z_inv_ref, xi_ref, yi_ref, zi_ref):
    n = BRICK
    w = 2 * n
    exp_index = lax.axis_index("exp")

    sz, sx, sy = (shift_ref[0, i] + n for i in range(3))
    moved = lax.rem(sx, n)
    turned = jnp.concatenate([x_inv_ref[0, pl.ds(moved, n), :], x_inv_ref[1, pl.ds(moved, n), :]], axis=0)
    high, low = split(turned)
    xi_ref[...] = jnp.concatenate([high, low], axis=1)[:, : 3 * n]
    lane = lax.broadcasted_iota(jnp.int32, (n, w), 1)
    back = lax.rem(w - lax.rem(sy, n), w)
    for ri_out in range(2):
        turned = pltpu.roll(y_inv_ref[ri_out], back, 1)
        pieces = []
        for ri in range(2):
            piece = turned[ri * n : (ri + 1) * n]
            pieces += [jnp.where(lane < n, piece, 0.0), jnp.where(lane < n, 0.0, piece)]
        high, low = split(jnp.concatenate(pieces, axis=0))
        at = slice(ri_out * w, (ri_out + 1) * w)
        yi_ref[0 : 2 * w, at] = high
        yi_ref[2 * w : 4 * w, at] = high
        yi_ref[4 * w :, at] = low
    first = lax.rem(HALF * exp_index + sz, n)
    turned = [jnp.concatenate([z_inv_ref[p, h, pl.ds(first, HALF), :] for h in range(2)], axis=1) for p in range(2)]
    turned = jnp.concatenate(turned, axis=0)
    high, low = split(turned)
    col = lax.broadcasted_iota(jnp.int32, turned.shape, 1)
    zi_ref[...] = jnp.where(col < 4 * GROUPS, high.astype(f32), low.astype(f32)).astype(bf16)[:, : 6 * GROUPS]


def prepare(
    own_ref, other_ref, pad_own_ref, pad_other_ref, first_ref, pack_ref, high_ref, raw_ref,
    *, bricks_y,
):
    n = BRICK
    w = 2 * n
    part = lax.axis_index("depth") // bricks_y
    columns = n + 2 * MARGIN
    pad = MARGIN * n
    strip = own_ref.shape[1]

    raw_ref[0:4, 0:pad] = pad_own_ref[0]
    raw_ref[4:8, 0:pad] = pad_other_ref[0]
    raw_ref[0:4, pad : pad + strip] = own_ref[...]
    reach = other_ref.shape[1]
    at = pad + part * (strip - reach) if reach < strip else pad
    raw_ref[4:8, pl.ds(pl.multiple_of(at, pad), reach)] = other_ref[...]
    raw_ref[0:4, pad + strip :] = pad_own_ref[pad_own_ref.shape[0] - 1]
    raw_ref[4:8, pad + strip :] = pad_other_ref[pad_other_ref.shape[0] - 1]
    row = lax.broadcasted_iota(jnp.int32, (8, w), 0)
    lane = lax.broadcasted_iota(jnp.int32, (8, w), 1)
    same = (row < 4) == (lane < n)
    swap = lambda v: pltpu.roll(v, n, 1)
    ratio = jnp.log(raw_ref[:, pl.ds(pl.multiple_of(part * (n * n), n * n), columns * n)])
    even, odd = [], []
    for k in range(columns // 2):
        here = ratio[:, k * w : (k + 1) * w]
        flipped = pltpu.roll(here, 4, 0)
        even.append(jnp.where(same, here, swap(flipped)))
        odd.append(jnp.where(same, swap(here), flipped))
    cols = []
    for k in range(columns // 2):
        cols += [even[k], jnp.where(row < 4, odd[k], odd[(k + 1) % (columns // 2)])]
    cols = jnp.concatenate(cols, axis=1)
    first_ref[...] = cols
    pack(cols, pack_ref, high_ref)


def kernel(
    tab_ref, first_ref, pack_in_ref, high_in_ref, xi_ref, yi_ref, zi_ref, z_fwd_ref, y_fwd_ref, x_fwd_ref,
    out_hbm,
    pack_ref, high_ref, shifted_ref, spec_ref, freq_ref, cross_ref,
    wave_ref, line_ref, back_ref, forward_ref,
    out_ref, out_sem,
):
    n = BRICK
    w = 2 * n
    exp_index = lax.axis_index("exp")

    tab = tab_ref[...]
    rows = lax.broadcasted_iota(jnp.int32, (8, w), 0)
    offs = jnp.where(rows < 4, tab, pltpu.roll(tab, 4, 0))
    frac = jnp.where(rows < 4, pltpu.roll(tab, 4, 0), tab)
    total = sum(tent_value(float(d), frac) for d in range(-2, 4))
    parity = (rows >= 4).astype(f32)
    blocks = [tent_value(SHIFT_LOW + 2 * q + parity - offs, frac) / total for q in range(PAIRS)]
    sums = jnp.sum(sum(blocks)[:, :n], axis=1, keepdims=True) / n
    uniform = jnp.log(sums + pltpu.roll(jnp.broadcast_to(sums, (8, w)), 4, 0)[:, :1])
    faint = jnp.exp(-jnp.sum(sum(blocks) * uniform, axis=0, keepdims=True) / 4.0)
    both_high, back_low = [], []
    for block in blocks:
        high, low = split(block / 4.0)
        both_high += [high.astype(f32)] * 2
        back_low.append(low.astype(f32))
    stacked = jnp.concatenate(both_high + back_low + [jnp.zeros((40, w), f32)], axis=0)
    back_ref[...] = jnp.transpose(stacked)[:n, :224].astype(bf16)
    high, low = split(jnp.concatenate(blocks, axis=0) * (faint / n))
    forward_ref[...] = jnp.concatenate([high, low], axis=1)[:, : 3 * n]

    swap = lambda v: pltpu.roll(v, n, 1)

    def spread(pack_from, high_from, first_lane, count):
        pieces = [pack_from[:, pl.ds(first_lane + 2 * w * q, count)] for q in range(PAIRS)]
        pieces += [high_from[:, pl.ds(first_lane + 2 * w * q, count)] for q in range(0, PAIRS, 2)]
        return jnp.concatenate(pieces, axis=0)

    lo_x, hi_x = -REACH, n + REACH
    chunk = 20 * w
    back_w = back_ref[...]
    forward_w = forward_ref[...]

    def first_pass(i, _):
        start = pl.multiple_of(i * chunk, 2 * w)
        logv = dot(back_w, spread(pack_in_ref, high_in_ref, start + (lo_x + SHIFT_LOW + MARGIN) * w, chunk))
        high, low = split(jnp.exp(logv))
        shifted_ref[:, pl.ds(start, chunk)] = dot(forward_w, jnp.concatenate([high, low, high], axis=0))
        return 0

    lax.fori_loop(0, (hi_x - lo_x) * w // chunk, first_pass, 0)

    lo_u, hi_u = -10, n + 10
    count = (hi_u - lo_u) * w
    gathered = sum(
        shifted_ref[8 * q : 8 * q + 8, pl.ds((lo_u - SHIFT_LOW - 2 * q - lo_x) * w, count)] for q in range(PAIRS)
    )
    proj = gathered[:, 2 * w :] + pltpu.roll(gathered[:, w : count - w], 4, 0)
    ratio = first_ref[:, (lo_u + 2 + MARGIN) * w : (hi_u + MARGIN) * w]
    ratio = (ratio - uniform) + (ratio - jnp.log(proj))
    later = pltpu.roll(jnp.concatenate([ratio[:, w:], ratio[:, :w]], axis=1), 4, 0)
    pack(jnp.where(lax.broadcasted_iota(jnp.int32, ratio.shape, 0) < 4, ratio, later), pack_ref, high_ref)

    per = 16
    chunk2 = per * w

    def second_pass(i, _):
        start = pl.multiple_of(i * chunk2, chunk2)
        logv = dot(back_w, spread(pack_ref, high_ref, start, chunk2))
        high, low = split(jnp.exp(logv))
        spec = dot(z_fwd_ref[...], jnp.concatenate([high, low, high], axis=0))
        groups = []
        for j in range(per):
            piece = spec[:, w * j : w * (j + 1)]
            groups.append(jnp.concatenate([piece[:ROWS], piece[ROWS:]], axis=1))
        high, low = split(jnp.concatenate(groups, axis=0))
        lines = dot(jnp.concatenate([high, low, high], axis=1), y_fwd_ref[...])
        at = pl.multiple_of(i * (per * ROWS), per * ROWS)
        spec_ref[0, pl.ds(at, per * ROWS), :] = lines[:, :w]
        spec_ref[1, pl.ds(at, per * ROWS), :] = lines[:, w:]
        return 0

    lax.fori_loop(0, n // per, second_pass, 0)

    lane = lax.broadcasted_iota(jnp.int32, (n, w), 1)
    row = lax.broadcasted_iota(jnp.int32, (n, w), 0)
    own_sign = jnp.where(exp_index == 0, 1.0, -1.0)
    exp_sign = jnp.where(lane < n, own_sign, -own_sign)
    anchor = (lane == 0) & (row == 0)

    def three(value):
        high, low = split(value)
        return jnp.concatenate([high, low, high], axis=0)

    def spectra(i, _):
        for t in range(UNROLL):
            at = jnp.maximum(i - 2, 0) * UNROLL + t
            both = dot(xi_ref[...], cross_ref[t])
            re = both[:n, :w] - both[n:, w:]
            im = both[:n, w:] + both[n:, :w]
            high, low = split(jnp.concatenate([re, im], axis=1))
            wave_ref[0, pl.ds(pl.multiple_of(at * n, n), n), :] = high
            wave_ref[1, pl.ds(pl.multiple_of(at * n, n), n), :] = low
        for t in range(UNROLL):
            re_a, im_a = freq_ref[t, 0, 0], freq_ref[t, 0, 1]
            re_b, im_b = freq_ref[t, 1, 0], freq_ref[t, 1, 1]
            re_one = jnp.where(lane < n, re_a, re_b)
            im_one = jnp.where(lane < n, im_a, im_b)
            re_two = swap(jnp.where(lane < n, re_b, re_a))
            im_two = swap(jnp.where(lane < n, im_b, im_a))
            power = (re_one * re_one + im_one * im_one) * (re_two * re_two + im_two * im_two)
            gain = lax.rsqrt(jnp.maximum(power, spectral_floor * spectral_floor))
            if t == 0:
                gain = jnp.where(anchor & (i == 1), 0.0, gain)
            cross_re = (re_one * re_two + im_one * im_two) * gain
            cross_im = (re_one * im_two - im_one * re_two) * (gain * exp_sign)
            cross_ref[t] = three(jnp.concatenate([cross_re, cross_im], axis=1))
        for t in range(UNROLL):
            for odd in range(2):
                kz = jnp.minimum(i, STEPS - 1) * (2 * UNROLL) + 2 * t + odd
                lines = [spec_ref[ri, pl.ds(kz, n, stride=ROWS), :] for ri in range(2)]
                both = dot(x_fwd_ref[...], three(jnp.concatenate(lines, axis=1)))
                freq_ref[t, odd, 0] = both[:n, :w] + both[n:, w:]
                freq_ref[t, odd, 1] = both[:n, w:] - both[n:, :w]
        return 0

    lax.fori_loop(0, STEPS + 2, spectra, 0)

    done = STEPS * UNROLL
    per = done // 2

    def inverse_y(i, _):
        at = pl.multiple_of(i * (per * n), per * n)
        high, low = wave_ref[0, pl.ds(at, per * n), :], wave_ref[1, pl.ds(at, per * n), :]
        lines = dot(jnp.concatenate([high, low, high], axis=1), yi_ref[...])
        for t in range(per):
            to = pl.multiple_of((i * per + t) * GAP, 8)
            line_ref[0, pl.ds(to, n), :] = lines[t * n : (t + 1) * n, :w]
            line_ref[1, pl.ds(to, n), :] = lines[t * n : (t + 1) * n, w:]
        return 0

    lax.fori_loop(0, 2, inverse_y, 0)
    line_ref[:, done * GAP :, :] = jnp.zeros((2, (GROUPS - done) * GAP, w), f32)

    lane = lax.broadcasted_iota(jnp.int32, (HALF, w), 1)
    x_per_step = 8

    def planes(i, _):
        for t in range(x_per_step):
            pair = i * x_per_step + t
            cols = jnp.concatenate(
                [
                    jnp.concatenate([line_ref[ri, pl.ds(2 * pair + p, GROUPS, stride=GAP), :] for ri in range(2)], axis=0)
                    for p in range(2)
                ],
                axis=1,
            )
            both = dot(zi_ref[...], three(cols))
            a_even, a_odd = both[:HALF, :w], both[:HALF, w:]
            b_even, b_odd = both[HALF:, :w], both[HALF:, w:]
            value = jnp.where(lane < n, a_even, b_odd) + swap(jnp.where(lane < n, a_odd, b_even))
            out_ref[:, pl.ds(pl.multiple_of(pair * w, w), w)] = value
        out_copy(i).start()
        return 0

    def out_copy(i):
        at = pl.ds(pl.multiple_of(i * (x_per_step * w), x_per_step * w), x_per_step * w)
        return pltpu.make_async_copy(out_ref.at[:, at], out_hbm.at[:, at], out_sem.at[i])

    lax.fori_loop(0, HALF // x_per_step, planes, 0)
    for i in range(HALF // x_per_step):
        out_copy(i).wait()


def share_tables(offsets, fractions):
    both = jnp.concatenate([offsets.astype(f32), fractions], axis=0)
    count = lax.axis_size("depth")
    slab = both.shape[1]
    lane = jnp.arange(2 * count * slab, dtype=jnp.int32) % (count * slab)
    mine = (lane // slab == lax.axis_index("depth")).astype(f32)
    table = jnp.tile(both, (1, 2 * count)) * mine
    step = count // 2
    while step > 2:
        table = table + lax.ppermute(table, "depth", [(i, i ^ step) for i in range(count)])
        step //= 2
    total = table
    for k in (1, 2, 3):
        total = total + lax.ppermute(table, "depth", [(i, i ^ k) for i in range(count)])
    return total


def windows(images, bricks_x, bricks_y):
    exps, tiles, depths = (lax.axis_size(a) for a in ("exp", "tile", "depth"))
    depth_index = lax.axis_index("depth")
    cams = images.shape[1]
    strip = lax.dynamic_slice_in_dim(images[0], depth_index % bricks_y * BRICK, BRICK, axis=2).reshape(cams, -1)

    def linear(e, t, d):
        return ((e % exps) * tiles + t % tiles) * depths + d

    def edge(step, other):
        edge_part = 0 if step == 1 else bricks_x - 1
        return [
            (linear(e, t, d), linear(e + other, t + step, d))
            for e in range(exps)
            for t in range(tiles)
            for d in range(depths)
            if d // bricks_y == edge_part
        ]

    axes = ("exp", "tile", "depth")
    tail = strip[:, -MARGIN * BRICK :]
    head = strip[:, : MARGIN * BRICK]
    pads = []
    for other in (0, 1):
        if bricks_x > 1:
            sent = jnp.where(depth_index // bricks_y == 0, tail, head)
            pads.append(lax.ppermute(sent, axes, edge(1, other) + edge(-1, other))[None])
        else:
            sides = ((tail, 1), (head, -1))
            pads.append(jnp.stack([lax.ppermute(v, axes, edge(step, other)) for v, step in sides]))
    piece = strip
    if bricks_x == 2:
        near = strip.shape[1] - MARGIN * BRICK
        piece = jnp.where(depth_index // bricks_y == 0, strip[:, :near], strip[:, -near:])
    other_strip = lax.ppermute(piece, "exp", [(i, (i + 1) % exps) for i in range(exps)])
    return strip, other_strip, pads[0], pads[1]


def per_device(images, offsets, fractions, shifts):
    cams, width, rows_y = images.shape[1:]
    bricks_x, bricks_y = width // BRICK, rows_y // BRICK
    assert cams == 4 and width % BRICK == 0 and rows_y % BRICK == 0
    assert bricks_x * bricks_y == lax.axis_size("depth")
    assert offsets.shape[1] * lax.axis_size("depth") == BRICK
    n = BRICK
    table = share_tables(offsets, fractions)
    strips = windows(images, bricks_x, bricks_y)
    window = (n + 2 * MARGIN) * n
    extended = (width + 2 * MARGIN) * n
    vmem = pl.BlockSpec(memory_space=pltpu.VMEM)
    z_fwd, y_fwd, x_fwd, *inverses = (jnp.asarray(v) for v in constant_tables())
    turned = pl.pallas_call(
        turn,
        out_shape=[
            jax.ShapeDtypeStruct((2 * n, 3 * n), bf16),
            jax.ShapeDtypeStruct((12 * n, 4 * n), bf16),
            jax.ShapeDtypeStruct((n, 6 * GROUPS), bf16),
        ],
        in_specs=[pl.BlockSpec(memory_space=pltpu.SMEM)] + [vmem] * 3,
        out_specs=[vmem] * 3,
        compiler_params=pltpu.CompilerParams(vmem_limit_bytes=8 * 1024 * 1024),
    )(shifts, *inverses)
    ready = pl.pallas_call(
        functools.partial(prepare, bricks_y=bricks_y),
        out_shape=[
            jax.ShapeDtypeStruct((8, 2 * window), f32),
            jax.ShapeDtypeStruct((16, 2 * window), bf16),
            jax.ShapeDtypeStruct((16, 2 * window), bf16),
        ],
        in_specs=[vmem] * 4,
        out_specs=[vmem] * 3,
        scratch_shapes=[pltpu.VMEM((8, extended), f32)],
        compiler_params=pltpu.CompilerParams(vmem_limit_bytes=16 * 1024 * 1024),
    )(*strips)
    second = (n + 18) * 2 * n
    out = pl.pallas_call(
        kernel,
        out_shape=jax.ShapeDtypeStruct((HALF, n * n), f32),
        in_specs=[vmem] * 10,
        out_specs=pl.BlockSpec(memory_space=pl.ANY),
        scratch_shapes=[
            pltpu.VMEM((16, second), bf16),
            pltpu.VMEM((16, second), bf16),
            pltpu.VMEM((8 * PAIRS, (n + 2 * REACH) * 2 * n), f32),
            pltpu.VMEM((2, n * ROWS, 2 * n), f32),
            pltpu.VMEM((UNROLL, 2, 2, n, 2 * n), f32),
            pltpu.VMEM((UNROLL, 3 * n, 4 * n), bf16),
            pltpu.VMEM((2, STEPS * UNROLL * n, 4 * n), bf16),
            pltpu.VMEM((2, GROUPS * GAP, 2 * n), f32),
            pltpu.VMEM((n, 224), bf16),
            pltpu.VMEM((8 * PAIRS, 3 * n), bf16),
            pltpu.VMEM((HALF, n * n), f32),
            pltpu.SemaphoreType.DMA((4,)),
        ],
        compiler_params=pltpu.CompilerParams(vmem_limit_bytes=40 * 1024 * 1024),
    )(table, *ready, *turned, z_fwd, y_fwd, x_fwd)
    return out.reshape(1, HALF, n * n)


def solution(mesh):
    placed = (
        P("exp", None, "tile", None),
        P(None, "depth"),
        P(None, "depth"),
        P(("tile", "depth"), None),
    )
    return jax.shard_map(
        per_device,
        mesh=mesh,
        in_specs=placed,
        out_specs=P(("tile", "depth"), "exp", None),
        check_vma=False,
    )
```

```python
import functools
import math

import jax
import jax.numpy as jnp
import numpy as np
from jax import lax
from jax.experimental import pallas as pl
from jax.experimental.pallas import tpu as pltpu
from jax.sharding import PartitionSpec as P


BRICK = 64
HALF = BRICK // 2
ROWS = 40
MARGIN = 32
SHIFT_LOW = -8
PAIRS = 9
REACH = 18
UNROLL = 2
STEPS = 8
PLANES = 18
GROUPS = 24
GAP = 72
spectral_floor = 0.01
f32, bf16 = jnp.float32, jnp.bfloat16


def split(value):
    high = value.astype(bf16)
    return high, (value - high.astype(f32)).astype(bf16)


def dot(a, b):
    return jnp.dot(a, b, preferred_element_type=f32)


def tent_value(distance, fraction):
    return jnp.maximum(0.0, 1.0 - jnp.abs(distance - fraction) / 1.5)


def dft_parts():
    wave = np.arange(BRICK)
    angle = (wave[:, None] * wave[None, :] % BRICK) * (2.0 * math.pi / BRICK)
    return np.cos(angle) / math.sqrt(BRICK), np.sin(angle) / math.sqrt(BRICK)


def host_split(value):
    high = value.astype(np.float32).astype(bf16)
    return high, (value - high.astype(np.float64)).astype(np.float32).astype(bf16)


def constant_tables():
    c, s = dft_parts()
    n = BRICK
    high, low = host_split(np.concatenate([c[: HALF + 1], -s[1:HALF]], axis=0))
    z_fwd = np.concatenate([high, high, low], axis=1)
    yt = np.zeros((2, 2, n, 2, 2, n))
    for e in range(2):
        yt[0, e, :, 0, e], yt[0, e, :, 1, e] = c, -s
        yt[1, e, :, 0, e], yt[1, e, :, 1, e] = s, c
    high, low = host_split(yt.reshape(4 * n, 4 * n))
    y_fwd = np.concatenate([high, high, low], axis=0)
    fold = np.zeros((n, n))
    fold[:HALF, 1:HALF], fold[HALF, 1:HALF] = c[:HALF, 1:HALF], c[HALF, 1:HALF]
    fold[HALF + 1 :, HALF + 1 :] = s[1:HALF, 1:HALF]
    fold[0 : HALF + 1 : 2, 0] = fold[1:HALF:2, HALF] = c[0, 0]
    high, low = host_split(fold)
    x_fwd = np.concatenate([high, high, low], axis=1)
    twice = lambda t: np.concatenate([t, t], axis=0)
    y_inv = np.stack([np.concatenate([twice(c), twice(-s)], 1).T, np.concatenate([twice(s), twice(c)], 1).T])
    y_inv = y_inv.astype(np.float32)
    weight = np.zeros(2 * GROUPS)
    weight[: HALF + 1] = 2.0
    weight[0] = weight[HALF] = 1.0
    z_inv = []
    for odd in range(2):
        pick = np.concatenate([(t[:, : 2 * GROUPS] * weight)[:, odd::2] for t in (c, -s)], axis=1)
        whole = twice(np.pad(np.tile(pick, (1, 3)), ((0, 0), (0, 4 * n - 6 * GROUPS))))
        z_inv.append(np.stack([whole[:, : 2 * n], whole[:, 2 * n :]]))
    return z_fwd, y_fwd, x_fwd, y_inv, np.stack(z_inv).astype(np.float32)


def pack(both, pack_ref, high_ref):
    w = 2 * BRICK
    high = both.astype(bf16).astype(f32)
    pack_ref[...] = jnp.concatenate([high, both - high], axis=0).astype(bf16)
    later = jnp.concatenate([high[:, 2 * w :], high[:, : 2 * w]], axis=1)
    high_ref[...] = jnp.concatenate([high, later], axis=0).astype(bf16)


def turn(shift_ref, y_inv_ref, z_inv_ref, yi_ref, zi_ref):
    n = BRICK
    w = 2 * n
    exp_index = lax.axis_index("exp")

    sz, sy = shift_ref[0, 0] + n, shift_ref[0, 2] + n
    lane = lax.broadcasted_iota(jnp.int32, (n, w), 1)
    back = lax.rem(w - lax.rem(sy, n), w)
    for ri_out in range(2):
        turned = pltpu.roll(y_inv_ref[ri_out], back, 1)
        pieces = []
        for ri in range(2):
            piece = turned[ri * n : (ri + 1) * n]
            pieces += [jnp.where(lane < n, piece, 0.0), jnp.where(lane < n, 0.0, piece)]
        high, low = split(jnp.concatenate(pieces, axis=0))
        at = slice(ri_out * w, (ri_out + 1) * w)
        yi_ref[0 : 2 * w, at] = high
        yi_ref[2 * w : 4 * w, at] = high
        yi_ref[4 * w :, at] = low
    first = lax.rem(HALF * exp_index + sz, n)
    turned = [jnp.concatenate([z_inv_ref[p, h, pl.ds(first, HALF), :] for h in range(2)], axis=1) for p in range(2)]
    turned = jnp.concatenate(turned, axis=0)
    high, low = split(turned)
    col = lax.broadcasted_iota(jnp.int32, turned.shape, 1)
    zi_ref[...] = jnp.where(col < 4 * GROUPS, high.astype(f32), low.astype(f32)).astype(bf16)[:, : 6 * GROUPS]


def prepare(
    own_ref, other_ref, pad_own_ref, pad_other_ref, first_ref, pack_ref, high_ref, raw_ref,
    *, bricks_y,
):
    n = BRICK
    w = 2 * n
    part = lax.axis_index("depth") // bricks_y
    columns = n + 2 * MARGIN
    pad = MARGIN * n
    strip = own_ref.shape[1]

    raw_ref[0:4, 0:pad] = pad_own_ref[0]
    raw_ref[4:8, 0:pad] = pad_other_ref[0]
    raw_ref[0:4, pad : pad + strip] = own_ref[...]
    reach = other_ref.shape[1]
    at = pad + part * (strip - reach) if reach < strip else pad
    raw_ref[4:8, pl.ds(pl.multiple_of(at, pad), reach)] = other_ref[...]
    raw_ref[0:4, pad + strip :] = pad_own_ref[pad_own_ref.shape[0] - 1]
    raw_ref[4:8, pad + strip :] = pad_other_ref[pad_other_ref.shape[0] - 1]
    row = lax.broadcasted_iota(jnp.int32, (8, w), 0)
    lane = lax.broadcasted_iota(jnp.int32, (8, w), 1)
    same = (row < 4) == (lane < n)
    swap = lambda v: pltpu.roll(v, n, 1)
    ratio = jnp.log(raw_ref[:, pl.ds(pl.multiple_of(part * (n * n), n * n), columns * n)])
    even, odd = [], []
    for k in range(columns // 2):
        here = ratio[:, k * w : (k + 1) * w]
        flipped = pltpu.roll(here, 4, 0)
        even.append(jnp.where(same, here, swap(flipped)))
        odd.append(jnp.where(same, swap(here), flipped))
    cols = []
    for k in range(columns // 2):
        cols += [even[k], jnp.where(row < 4, odd[k], odd[(k + 1) % (columns // 2)])]
    cols = jnp.concatenate(cols, axis=1)
    first_ref[...] = cols
    pack(cols, pack_ref, high_ref)


def kernel(
    shift_any, tab_ref, first_ref, pack_in_ref, high_in_ref, yi_ref, zi_ref, z_fwd_ref, y_fwd_ref, x_fwd_ref,
    out_hbm,
    pack_ref, high_ref, shifted_ref, spec_ref, edge_ref, freq_ref, cross_ref,
    wave_ref, line_ref, back_ref, forward_ref,
    out_ref, out_sem, shift_ref, shift_sem, place_ref,
):
    n = BRICK
    w = 2 * n
    exp_index = lax.axis_index("exp")

    shift_copy = pltpu.make_async_copy(shift_any, shift_ref, shift_sem)
    shift_copy.start()
    line_ref[:, PLANES * GAP :, :] = jnp.zeros((2, (GROUPS - PLANES) * GAP, w), f32)
    wave_ref[:, (PLANES - 1) * n :, :] = jnp.zeros((2, n, 2 * w), bf16)

    tab = tab_ref[...]
    rows = lax.broadcasted_iota(jnp.int32, (8, w), 0)
    offs = jnp.where(rows < 4, tab, pltpu.roll(tab, 4, 0))
    frac = jnp.where(rows < 4, pltpu.roll(tab, 4, 0), tab)
    total = sum(tent_value(float(d), frac) for d in range(-2, 4))
    parity = (rows >= 4).astype(f32)
    blocks = [tent_value(SHIFT_LOW + 2 * q + parity - offs, frac) / total for q in range(PAIRS)]
    sums = jnp.sum(sum(blocks)[:, :n], axis=1, keepdims=True) / n
    uniform = jnp.log(sums + pltpu.roll(jnp.broadcast_to(sums, (8, w)), 4, 0)[:, :1])
    faint = jnp.exp(-jnp.sum(sum(blocks) * uniform, axis=0, keepdims=True) / 4.0)
    both_high, back_low = [], []
    for block in blocks:
        high, low = split(block / 4.0)
        both_high += [high.astype(f32)] * 2
        back_low.append(low.astype(f32))
    stacked = jnp.concatenate(both_high + back_low + [jnp.zeros((40, w), f32)], axis=0)
    back_ref[...] = jnp.transpose(stacked)[:n, :224].astype(bf16)
    high, low = split(jnp.concatenate(blocks, axis=0) * (faint / n))
    forward_ref[...] = jnp.concatenate([high, low], axis=1)[:, : 3 * n]

    swap = lambda v: pltpu.roll(v, n, 1)

    def spread(pack_from, high_from, first_lane, count):
        pieces = [pack_from[:, pl.ds(first_lane + 2 * w * q, count)] for q in range(PAIRS)]
        pieces += [high_from[:, pl.ds(first_lane + 2 * w * q, count)] for q in range(0, PAIRS, 2)]
        return jnp.concatenate(pieces, axis=0)

    lo_x, hi_x = -REACH, n + REACH
    chunk = 20 * w
    back_w = back_ref[...]
    forward_w = forward_ref[...]

    def first_pass(i, _):
        start = pl.multiple_of(i * chunk, 2 * w)
        logv = dot(back_w, spread(pack_in_ref, high_in_ref, start + (lo_x + SHIFT_LOW + MARGIN) * w, chunk))
        high, low = split(jnp.exp(logv))
        shifted_ref[:, pl.ds(start, chunk)] = dot(forward_w, jnp.concatenate([high, low, high], axis=0))
        return 0

    lax.fori_loop(0, (hi_x - lo_x) * w // chunk, first_pass, 0)

    lo_u, hi_u = -10, n + 10
    count = (hi_u - lo_u) * w
    gathered = sum(
        shifted_ref[8 * q : 8 * q + 8, pl.ds((lo_u - SHIFT_LOW - 2 * q - lo_x) * w, count)] for q in range(PAIRS)
    )
    proj = gathered[:, 2 * w :] + pltpu.roll(gathered[:, w : count - w], 4, 0)
    ratio = first_ref[:, (lo_u + 2 + MARGIN) * w : (hi_u + MARGIN) * w]
    ratio = (ratio - uniform) + (ratio - jnp.log(proj))
    later = pltpu.roll(jnp.concatenate([ratio[:, w:], ratio[:, :w]], axis=1), 4, 0)
    pack(jnp.where(lax.broadcasted_iota(jnp.int32, ratio.shape, 0) < 4, ratio, later), pack_ref, high_ref)

    top = lax.broadcasted_iota(jnp.int32, (8, w), 0) == 0
    place = lambda x: jnp.where(x <= HALF, x, n + HALF - x)

    per = 16
    chunk2 = per * w

    def second_pass(i, _):
        start = pl.multiple_of(i * chunk2, chunk2)
        logv = dot(back_w, spread(pack_ref, high_ref, start, chunk2))
        high, low = split(jnp.exp(logv))
        spec = dot(z_fwd_ref[...], jnp.concatenate([high, low, high], axis=0))
        groups = []
        for j in range(per):
            piece = spec[:, w * j : w * (j + 1)]
            imag = jnp.concatenate([jnp.where(top, 0.0, piece[HALF : HALF + 8]), piece[HALF + 8 :]], axis=0)
            groups.append(jnp.concatenate([piece[:HALF], imag], axis=1))
            edge_ref[0, pl.ds(place(i * per + j), 1), :] = piece[HALF : HALF + 1]
        high, low = split(jnp.concatenate(groups, axis=0))
        lines = dot(jnp.concatenate([high, low, high], axis=1), y_fwd_ref[...])
        for j in range(per):
            at = pl.multiple_of(place(i * per + j) * ROWS, ROWS)
            spec_ref[0, pl.ds(at, HALF), :] = lines[j * HALF : (j + 1) * HALF, :w]
            spec_ref[1, pl.ds(at, HALF), :] = lines[j * HALF : (j + 1) * HALF, w:]
        return 0

    lax.fori_loop(0, n // per, second_pass, 0)
    high, low = split(jnp.concatenate([edge_ref[0], jnp.zeros((n, w), f32)], axis=1))
    lines = dot(jnp.concatenate([high, low, high], axis=1), y_fwd_ref[...])
    edge_ref[0], edge_ref[1] = lines[:, :w], lines[:, w:]

    lane = lax.broadcasted_iota(jnp.int32, (n, w), 1)
    row = lax.broadcasted_iota(jnp.int32, (n, w), 0)
    own_sign = jnp.where(exp_index == 0, 1.0, -1.0)
    exp_sign = jnp.where(lane < n, own_sign, -own_sign)
    anchor = (lane == 0) & (row == 0)

    def three(value):
        high, low = split(value)
        return jnp.concatenate([high, low, high], axis=0)

    def folded(pieces):
        value = jnp.concatenate(pieces, axis=1)
        return three(jnp.concatenate([value[:HALF] + value[HALF:], value[:HALF] - value[HALF:]], axis=0))

    def unfolded(both, sign):
        cos_re, cos_im, sin_re, sin_im = (both[r : r + HALF, c : c + w] for r in (0, HALF) for c in (0, w))
        re, re_mirror = cos_re - sin_im, cos_re + sin_im
        im, im_mirror = cos_im + sin_re, cos_im - sin_re
        if sign < 0:
            re, re_mirror, im, im_mirror = re_mirror, re, im_mirror, im
        pieces = []
        for plain, mirror, cos_part, sin_part in ((re, re_mirror, cos_re, sin_re), (im, im_mirror, cos_im, sin_im)):
            first = [jnp.where(top, cos_part[:8], plain[:8]), plain[8:]]
            pieces.append(jnp.concatenate(first + [jnp.where(top, sin_part[:8], mirror[:8]), mirror[8:]], axis=0))
        return pieces

    def columns_to_spectrum(i):
        for t in range(UNROLL):
            for odd in range(2):
                kz = i * (2 * UNROLL) + 2 * t + odd
                lines = [spec_ref[ri, pl.ds(kz, n, stride=ROWS), :] for ri in range(2)]
                freq_ref[t, odd, 0], freq_ref[t, odd, 1] = unfolded(dot(x_fwd_ref[...], folded(lines)), -1.0)

    def last_to_spectrum():
        freq_ref[0, 0, 0], freq_ref[0, 0, 1] = unfolded(dot(x_fwd_ref[...], folded([edge_ref[0], edge_ref[1]])), -1.0)
        freq_ref[0, 1] = jnp.zeros((2, n, w), f32)

    def spectrum_to_cross(holds_anchor, count=UNROLL):
        for t in range(count):
            re_a, im_a = freq_ref[t, 0, 0], freq_ref[t, 0, 1]
            re_b, im_b = freq_ref[t, 1, 0], freq_ref[t, 1, 1]
            re_one = jnp.where(lane < n, re_a, re_b)
            im_one = jnp.where(lane < n, im_a, im_b)
            re_two = swap(jnp.where(lane < n, re_b, re_a))
            im_two = swap(jnp.where(lane < n, im_b, im_a))
            cross_re = re_one * re_two + im_one * im_two
            cross_im = re_one * im_two - im_one * re_two
            power = cross_re * cross_re + cross_im * cross_im
            gain = lax.rsqrt(jnp.maximum(power, spectral_floor * spectral_floor))
            if holds_anchor and t == 0:
                gain = jnp.where(anchor, 0.0, gain)
            cross_re, cross_im = cross_re * gain, cross_im * (gain * exp_sign)
            cross_ref[t] = folded([cross_re, cross_im])

    def cross_to_wave(i, count=UNROLL):
        for t in range(count):
            at = i * UNROLL + t
            high, low = split(jnp.concatenate(unfolded(dot(x_fwd_ref[...], cross_ref[t]), 1.0), axis=1))
            wave_ref[0, pl.ds(pl.multiple_of(at * n, n), n), :] = high
            wave_ref[1, pl.ds(pl.multiple_of(at * n, n), n), :] = low

    def spectra(i, _):
        cross_to_wave(i - 2)
        spectrum_to_cross(False)
        columns_to_spectrum(i)
        return 0

    shift_copy.wait()
    for x in range(n):
        place_ref[x] = place(lax.rem(shift_ref[0, 1] + (n + x), n))
    columns_to_spectrum(0)
    spectrum_to_cross(True)
    columns_to_spectrum(1)
    lax.fori_loop(2, STEPS, spectra, 0)
    cross_to_wave(STEPS - 2)
    spectrum_to_cross(False)
    last_to_spectrum()
    cross_to_wave(STEPS - 1)
    spectrum_to_cross(False, 1)
    cross_to_wave(STEPS, 1)

    done = PLANES
    per = done // 2

    def inverse_y(i, _):
        at = pl.multiple_of(i * (per * n), per * n)
        high, low = wave_ref[0, pl.ds(at, per * n), :], wave_ref[1, pl.ds(at, per * n), :]
        lines = dot(jnp.concatenate([high, low, high], axis=1), yi_ref[...])
        for t in range(per):
            to = pl.multiple_of((i * per + t) * GAP, 8)
            line_ref[0, pl.ds(to, n), :] = lines[t * n : (t + 1) * n, :w]
            line_ref[1, pl.ds(to, n), :] = lines[t * n : (t + 1) * n, w:]
        return 0

    lax.fori_loop(0, 2, inverse_y, 0)

    lane = lax.broadcasted_iota(jnp.int32, (HALF, w), 1)
    x_per_step = 16

    def planes(i, _):
        for t in range(x_per_step):
            pair = i * x_per_step + t
            cols = jnp.concatenate(
                [
                    jnp.concatenate([line_ref[ri, pl.ds(place_ref[2 * pair + p], GROUPS, stride=GAP), :] for ri in range(2)], axis=0)
                    for p in range(2)
                ],
                axis=1,
            )
            both = dot(zi_ref[...], three(cols))
            a_even, a_odd = both[:HALF, :w], both[:HALF, w:]
            b_even, b_odd = both[HALF:, :w], both[HALF:, w:]
            value = jnp.where(lane < n, a_even, b_odd) + swap(jnp.where(lane < n, a_odd, b_even))
            out_ref[:, pl.ds(pl.multiple_of(pair * w, w), w)] = value
        out_copy(i).start()
        return 0

    def out_copy(i):
        at = pl.ds(pl.multiple_of(i * (x_per_step * w), x_per_step * w), x_per_step * w)
        return pltpu.make_async_copy(out_ref.at[:, at], out_hbm.at[:, at], out_sem.at[i])

    lax.fori_loop(0, HALF // x_per_step, planes, 0)
    for i in range(HALF // x_per_step):
        out_copy(i).wait()


def share_tables(offsets, fractions):
    both = jnp.concatenate([offsets.astype(f32), fractions], axis=0)
    count = lax.axis_size("depth")
    slab = both.shape[1]
    lane = jnp.arange(2 * count * slab, dtype=jnp.int32) % (count * slab)
    mine = (lane // slab == lax.axis_index("depth")).astype(f32)
    table = jnp.tile(both, (1, 2 * count)) * mine
    step = count // 2
    while step > 2:
        table = table + lax.ppermute(table, "depth", [(i, i ^ step) for i in range(count)])
        step //= 2
    total = table
    for k in (1, 2, 3):
        total = total + lax.ppermute(table, "depth", [(i, i ^ k) for i in range(count)])
    return total


def windows(images, bricks_x, bricks_y):
    exps, tiles, depths = (lax.axis_size(a) for a in ("exp", "tile", "depth"))
    depth_index = lax.axis_index("depth")
    cams = images.shape[1]
    strip = lax.dynamic_slice_in_dim(images[0], depth_index % bricks_y * BRICK, BRICK, axis=2).reshape(cams, -1)

    def linear(e, t, d):
        return ((e % exps) * tiles + t % tiles) * depths + d

    def edge(step, other):
        edge_part = 0 if step == 1 else bricks_x - 1
        return [
            (linear(e, t, d), linear(e + other, t + step, d))
            for e in range(exps)
            for t in range(tiles)
            for d in range(depths)
            if d // bricks_y == edge_part
        ]

    axes = ("exp", "tile", "depth")
    tail = strip[:, -MARGIN * BRICK :]
    head = strip[:, : MARGIN * BRICK]
    pads = []
    for other in (0, 1):
        if bricks_x > 1:
            sent = jnp.where(depth_index // bricks_y == 0, tail, head)
            pads.append(lax.ppermute(sent, axes, edge(1, other) + edge(-1, other))[None])
        else:
            sides = ((tail, 1), (head, -1))
            pads.append(jnp.stack([lax.ppermute(v, axes, edge(step, other)) for v, step in sides]))
    piece = strip
    if bricks_x == 2:
        near = strip.shape[1] - MARGIN * BRICK
        piece = jnp.where(depth_index // bricks_y == 0, strip[:, :near], strip[:, -near:])
    other_strip = lax.ppermute(piece, "exp", [(i, (i + 1) % exps) for i in range(exps)])
    return strip, other_strip, pads[0], pads[1]


def per_device(images, offsets, fractions, shifts):
    cams, width, rows_y = images.shape[1:]
    bricks_x, bricks_y = width // BRICK, rows_y // BRICK
    assert cams == 4 and width % BRICK == 0 and rows_y % BRICK == 0
    assert bricks_x * bricks_y == lax.axis_size("depth")
    assert offsets.shape[1] * lax.axis_size("depth") == BRICK
    n = BRICK
    table = share_tables(offsets, fractions)
    strips = windows(images, bricks_x, bricks_y)
    window = (n + 2 * MARGIN) * n
    extended = (width + 2 * MARGIN) * n
    vmem = pl.BlockSpec(memory_space=pltpu.VMEM)
    z_fwd, y_fwd, x_fwd, *inverses = (jnp.asarray(v) for v in constant_tables())
    turned = pl.pallas_call(
        turn,
        out_shape=[
            jax.ShapeDtypeStruct((12 * n, 4 * n), bf16),
            jax.ShapeDtypeStruct((n, 6 * GROUPS), bf16),
        ],
        in_specs=[pl.BlockSpec(memory_space=pltpu.SMEM)] + [vmem] * 2,
        out_specs=[vmem] * 2,
        compiler_params=pltpu.CompilerParams(vmem_limit_bytes=8 * 1024 * 1024),
    )(shifts, *inverses)
    ready = pl.pallas_call(
        functools.partial(prepare, bricks_y=bricks_y),
        out_shape=[
            jax.ShapeDtypeStruct((8, 2 * window), f32),
            jax.ShapeDtypeStruct((16, 2 * window), bf16),
            jax.ShapeDtypeStruct((16, 2 * window), bf16),
        ],
        in_specs=[vmem] * 4,
        out_specs=[vmem] * 3,
        scratch_shapes=[pltpu.VMEM((8, extended), f32)],
        compiler_params=pltpu.CompilerParams(vmem_limit_bytes=16 * 1024 * 1024),
    )(*strips)
    second = (n + 18) * 2 * n
    out = pl.pallas_call(
        kernel,
        out_shape=jax.ShapeDtypeStruct((HALF, n * n), f32),
        in_specs=[pl.BlockSpec(memory_space=pl.ANY)] + [vmem] * 9,
        out_specs=pl.BlockSpec(memory_space=pl.ANY),
        scratch_shapes=[
            pltpu.VMEM((16, second), bf16),
            pltpu.VMEM((16, second), bf16),
            pltpu.VMEM((8 * PAIRS, (n + 2 * REACH) * 2 * n), f32),
            pltpu.VMEM((2, n * ROWS, 2 * n), f32),
            pltpu.VMEM((2, n, 2 * n), f32),
            pltpu.VMEM((UNROLL, 2, 2, n, 2 * n), f32),
            pltpu.VMEM((UNROLL, 3 * n, 4 * n), bf16),
            pltpu.VMEM((2, PLANES * n, 4 * n), bf16),
            pltpu.VMEM((2, GROUPS * GAP, 2 * n), f32),
            pltpu.VMEM((n, 224), bf16),
            pltpu.VMEM((8 * PAIRS, 3 * n), bf16),
            pltpu.VMEM((HALF, n * n), f32),
            pltpu.SemaphoreType.DMA((2,)),
            pltpu.SMEM(shifts.shape, jnp.int32),
            pltpu.SemaphoreType.DMA(()),
            pltpu.SMEM((n,), jnp.int32),
        ],
        compiler_params=pltpu.CompilerParams(vmem_limit_bytes=40 * 1024 * 1024),
    )(shifts, table, *ready, *turned, z_fwd, y_fwd, x_fwd)
    return out.reshape(1, HALF, n * n)


def solution(mesh):
    placed = (
        P("exp", None, "tile", None),
        P(None, "depth"),
        P(None, "depth"),
        P(("tile", "depth"), None),
    )
    return jax.shard_map(
        per_device,
        mesh=mesh,
        in_specs=placed,
        out_specs=P(("tile", "depth"), "exp", None),
        check_vma=False,
    )
```

```python
import functools
import math

import jax
import jax.numpy as jnp
import numpy as np
from jax import lax
from jax.experimental import pallas as pl
from jax.experimental.pallas import tpu as pltpu
from jax.sharding import PartitionSpec as P


BRICK = 64
HALF = BRICK // 2
ROWS = 40
MARGIN = 32
SHIFT_LOW = -8
PAIRS = 9
REACH = 18
UNROLL = 2
STEPS = 8
PLANES = 18
GROUPS = 24
GAP = 72
spectral_floor = 0.01
f32, bf16 = jnp.float32, jnp.bfloat16


def split(value):
    high = value.astype(bf16)
    return high, (value - high.astype(f32)).astype(bf16)


def dot(a, b):
    return jnp.dot(a, b, preferred_element_type=f32)


def tent_value(distance, fraction):
    return jnp.maximum(0.0, 1.0 - jnp.abs(distance - fraction) / 1.5)


def dft_parts():
    wave = np.arange(BRICK)
    angle = (wave[:, None] * wave[None, :] % BRICK) * (2.0 * math.pi / BRICK)
    return np.cos(angle) / math.sqrt(BRICK), np.sin(angle) / math.sqrt(BRICK)


def host_split(value):
    high = value.astype(np.float32).astype(bf16)
    return high, (value - high.astype(np.float64)).astype(np.float32).astype(bf16)


def constant_tables():
    c, s = dft_parts()
    n = BRICK
    high, low = host_split(np.concatenate([c[: HALF + 1], -s[1:HALF]], axis=0))
    z_fwd = np.concatenate([high, high, low], axis=1)
    yt = np.zeros((2, 2, n, 2, 2, n))
    for e in range(2):
        yt[0, e, :, 0, e], yt[0, e, :, 1, e] = c, -s
        yt[1, e, :, 0, e], yt[1, e, :, 1, e] = s, c
    high, low = host_split(yt.reshape(4 * n, 4 * n))
    y_fwd = np.concatenate([high, high, low], axis=0)
    fold = np.zeros((n, n))
    fold[:HALF, 1:HALF], fold[HALF, 1:HALF] = c[:HALF, 1:HALF], c[HALF, 1:HALF]
    fold[HALF + 1 :, HALF + 1 :] = s[1:HALF, 1:HALF]
    fold[0 : HALF + 1 : 2, 0] = fold[1:HALF:2, HALF] = c[0, 0]
    high, low = host_split(fold)
    x_fwd = np.concatenate([high, high, low], axis=1)
    twice = lambda t: np.concatenate([t, t], axis=0)
    y_inv = np.stack([np.concatenate([twice(c), twice(-s)], 1).T, np.concatenate([twice(s), twice(c)], 1).T])
    y_inv = y_inv.astype(np.float32)
    weight = np.zeros(2 * GROUPS)
    weight[: HALF + 1] = 2.0
    weight[0] = weight[HALF] = 1.0
    z_inv = []
    for odd in range(2):
        pick = np.concatenate([(t[:, : 2 * GROUPS] * weight)[:, odd::2] for t in (c, -s)], axis=1)
        whole = twice(np.pad(np.tile(pick, (1, 3)), ((0, 0), (0, 4 * n - 6 * GROUPS))))
        z_inv.append(np.stack([whole[:, : 2 * n], whole[:, 2 * n :]]))
    return z_fwd, y_fwd, x_fwd, y_inv, np.stack(z_inv).astype(np.float32)


def pack(both, pack_ref, high_ref):
    w = 2 * BRICK
    high = both.astype(bf16).astype(f32)
    pack_ref[...] = jnp.concatenate([high, both - high], axis=0).astype(bf16)
    later = jnp.concatenate([high[:, 2 * w :], high[:, : 2 * w]], axis=1)
    high_ref[...] = jnp.concatenate([high, later], axis=0).astype(bf16)


def turn(shift_ref, y_inv_ref, z_inv_ref, yi_ref, zi_ref):
    n = BRICK
    w = 2 * n
    exp_index = lax.axis_index("exp")

    sz, sy = shift_ref[0, 0] + n, shift_ref[0, 2] + n
    lane = lax.broadcasted_iota(jnp.int32, (n, w), 1)
    back = lax.rem(w - lax.rem(sy, n), w)
    for ri_out in range(2):
        turned = pltpu.roll(y_inv_ref[ri_out], back, 1)
        pieces = []
        for ri in range(2):
            piece = turned[ri * n : (ri + 1) * n]
            pieces += [jnp.where(lane < n, piece, 0.0), jnp.where(lane < n, 0.0, piece)]
        high, low = split(jnp.concatenate(pieces, axis=0))
        at = slice(ri_out * w, (ri_out + 1) * w)
        yi_ref[0 : 2 * w, at] = high
        yi_ref[2 * w : 4 * w, at] = high
        yi_ref[4 * w :, at] = low
    first = lax.rem(HALF * exp_index + sz, n)
    turned = [jnp.concatenate([z_inv_ref[p, h, pl.ds(first, HALF), :] for h in range(2)], axis=1) for p in range(2)]
    turned = jnp.concatenate(turned, axis=0)
    high, low = split(turned)
    col = lax.broadcasted_iota(jnp.int32, turned.shape, 1)
    zi_ref[...] = jnp.where(col < 4 * GROUPS, high.astype(f32), low.astype(f32)).astype(bf16)[:, : 6 * GROUPS]


def prepare(
    own_ref, other_ref, pad_own_ref, pad_other_ref, first_ref, pack_ref, high_ref, raw_ref,
    *, bricks_y,
):
    n = BRICK
    w = 2 * n
    part = lax.axis_index("depth") // bricks_y
    columns = n + 2 * MARGIN
    pad = MARGIN * n
    strip = own_ref.shape[1]

    raw_ref[0:4, 0:pad] = pad_own_ref[0]
    raw_ref[4:8, 0:pad] = pad_other_ref[0]
    raw_ref[0:4, pad : pad + strip] = own_ref[...]
    reach = other_ref.shape[1]
    at = pad + part * (strip - reach) if reach < strip else pad
    raw_ref[4:8, pl.ds(pl.multiple_of(at, pad), reach)] = other_ref[...]
    raw_ref[0:4, pad + strip :] = pad_own_ref[pad_own_ref.shape[0] - 1]
    raw_ref[4:8, pad + strip :] = pad_other_ref[pad_other_ref.shape[0] - 1]
    row = lax.broadcasted_iota(jnp.int32, (8, w), 0)
    lane = lax.broadcasted_iota(jnp.int32, (8, w), 1)
    same = (row < 4) == (lane < n)
    swap = lambda v: pltpu.roll(v, n, 1)
    ratio = jnp.log(raw_ref[:, pl.ds(pl.multiple_of(part * (n * n), n * n), columns * n)])
    even, odd = [], []
    for k in range(columns // 2):
        here = ratio[:, k * w : (k + 1) * w]
        flipped = pltpu.roll(here, 4, 0)
        even.append(jnp.where(same, here, swap(flipped)))
        odd.append(jnp.where(same, swap(here), flipped))
    cols = []
    for k in range(columns // 2):
        cols += [even[k], jnp.where(row < 4, odd[k], odd[(k + 1) % (columns // 2)])]
    cols = jnp.concatenate(cols, axis=1)
    first_ref[...] = cols
    pack(cols, pack_ref, high_ref)


def kernel(
    shift_any, tab_ref, first_ref, pack_in_ref, high_in_ref, yi_ref, zi_ref, z_fwd_ref, y_fwd_ref, x_fwd_ref,
    out_hbm,
    pack_ref, high_ref, shifted_ref, spec_ref, edge_ref, freq_ref, cross_ref,
    wave_ref, line_ref, back_ref, forward_ref,
    out_ref, out_sem, shift_ref, shift_sem, place_ref,
):
    n = BRICK
    w = 2 * n
    exp_index = lax.axis_index("exp")

    shift_copy = pltpu.make_async_copy(shift_any, shift_ref, shift_sem)
    shift_copy.start()
    line_ref[:, PLANES * GAP :, :] = jnp.zeros((2, (GROUPS - PLANES) * GAP, w), f32)
    wave_ref[:, (PLANES - 1) * n :, :] = jnp.zeros((2, n, 2 * w), bf16)

    tab = tab_ref[...]
    rows = lax.broadcasted_iota(jnp.int32, (8, w), 0)
    offs = jnp.where(rows < 4, tab, pltpu.roll(tab, 4, 0))
    frac = jnp.where(rows < 4, pltpu.roll(tab, 4, 0), tab)
    total = sum(tent_value(float(d), frac) for d in range(-2, 4))
    parity = (rows >= 4).astype(f32)
    blocks = [tent_value(SHIFT_LOW + 2 * q + parity - offs, frac) / total for q in range(PAIRS)]
    sums = jnp.sum(sum(blocks)[:, :n], axis=1, keepdims=True) / n
    uniform = jnp.log(sums + pltpu.roll(jnp.broadcast_to(sums, (8, w)), 4, 0)[:, :1])
    faint = jnp.exp(-jnp.sum(sum(blocks) * uniform, axis=0, keepdims=True) / 4.0)
    both_high, back_low = [], []
    for block in blocks:
        high, low = split(block / 4.0)
        both_high += [high.astype(f32)] * 2
        back_low.append(low.astype(f32))
    stacked = jnp.concatenate(both_high + back_low + [jnp.zeros((40, w), f32)], axis=0)
    back_ref[...] = jnp.transpose(stacked)[:n, :224].astype(bf16)
    high, low = split(jnp.concatenate(blocks, axis=0) * (faint / n))
    forward_ref[...] = jnp.concatenate([high, low], axis=1)[:, : 3 * n]

    swap = lambda v: pltpu.roll(v, n, 1)

    def spread(pack_from, high_from, first_lane, count):
        pieces = [pack_from[:, pl.ds(first_lane + 2 * w * q, count)] for q in range(PAIRS)]
        pieces += [high_from[:, pl.ds(first_lane + 2 * w * q, count)] for q in range(0, PAIRS, 2)]
        return jnp.concatenate(pieces, axis=0)

    lo_x, hi_x = -REACH, n + REACH
    chunk = 100 * w
    back_w = back_ref[...]
    forward_w = forward_ref[...]

    def first_pass(i, _):
        start = pl.multiple_of(i * chunk, 2 * w)
        logv = dot(back_w, spread(pack_in_ref, high_in_ref, start + (lo_x + SHIFT_LOW + MARGIN) * w, chunk))
        high, low = split(jnp.exp(logv))
        shifted_ref[:, pl.ds(start, chunk)] = dot(forward_w, jnp.concatenate([high, low, high], axis=0))
        return 0

    lax.fori_loop(0, (hi_x - lo_x) * w // chunk, first_pass, 0)

    lo_u, hi_u = -10, n + 10
    count = (hi_u - lo_u) * w
    gathered = sum(
        shifted_ref[8 * q : 8 * q + 8, pl.ds((lo_u - SHIFT_LOW - 2 * q - lo_x) * w, count)] for q in range(PAIRS)
    )
    proj = gathered[:, 2 * w :] + pltpu.roll(gathered[:, w : count - w], 4, 0)
    ratio = first_ref[:, (lo_u + 2 + MARGIN) * w : (hi_u + MARGIN) * w]
    ratio = (ratio - uniform) + (ratio - jnp.log(proj))
    later = pltpu.roll(jnp.concatenate([ratio[:, w:], ratio[:, :w]], axis=1), 4, 0)
    pack(jnp.where(lax.broadcasted_iota(jnp.int32, ratio.shape, 0) < 4, ratio, later), pack_ref, high_ref)

    top = lax.broadcasted_iota(jnp.int32, (8, w), 0) == 0
    place = lambda x: jnp.where(x <= HALF, x, n + HALF - x)

    per = 64
    chunk2 = per * w

    def second_pass(i, _):
        start = pl.multiple_of(i * chunk2, chunk2)
        logv = dot(back_w, spread(pack_ref, high_ref, start, chunk2))
        high, low = split(jnp.exp(logv))
        spec = dot(z_fwd_ref[...], jnp.concatenate([high, low, high], axis=0))
        groups = []
        for j in range(per):
            piece = spec[:, w * j : w * (j + 1)]
            imag = jnp.concatenate([jnp.where(top, 0.0, piece[HALF : HALF + 8]), piece[HALF + 8 :]], axis=0)
            groups.append(jnp.concatenate([piece[:HALF], imag], axis=1))
            edge_ref[0, pl.ds(place(i * per + j), 1), :] = piece[HALF : HALF + 1]
        high, low = split(jnp.concatenate(groups, axis=0))
        lines = dot(jnp.concatenate([high, low, high], axis=1), y_fwd_ref[...])
        for j in range(per):
            at = pl.multiple_of(place(i * per + j) * ROWS, ROWS)
            spec_ref[0, pl.ds(at, HALF), :] = lines[j * HALF : (j + 1) * HALF, :w]
            spec_ref[1, pl.ds(at, HALF), :] = lines[j * HALF : (j + 1) * HALF, w:]
        return 0

    lax.fori_loop(0, n // per, second_pass, 0)
    high, low = split(jnp.concatenate([edge_ref[0], jnp.zeros((n, w), f32)], axis=1))
    lines = dot(jnp.concatenate([high, low, high], axis=1), y_fwd_ref[...])
    edge_ref[0], edge_ref[1] = lines[:, :w], lines[:, w:]

    lane = lax.broadcasted_iota(jnp.int32, (n, w), 1)
    row = lax.broadcasted_iota(jnp.int32, (n, w), 0)
    own_sign = jnp.where(exp_index == 0, 1.0, -1.0)
    exp_sign = jnp.where(lane < n, own_sign, -own_sign)
    anchor = (lane == 0) & (row == 0)

    def three(value):
        high, low = split(value)
        return jnp.concatenate([high, low, high], axis=0)

    def folded(pieces):
        value = jnp.concatenate(pieces, axis=1)
        return three(jnp.concatenate([value[:HALF] + value[HALF:], value[:HALF] - value[HALF:]], axis=0))

    def unfolded(both, sign):
        cos_re, cos_im, sin_re, sin_im = (both[r : r + HALF, c : c + w] for r in (0, HALF) for c in (0, w))
        re, re_mirror = cos_re - sin_im, cos_re + sin_im
        im, im_mirror = cos_im + sin_re, cos_im - sin_re
        if sign < 0:
            re, re_mirror, im, im_mirror = re_mirror, re, im_mirror, im
        pieces = []
        for plain, mirror, cos_part, sin_part in ((re, re_mirror, cos_re, sin_re), (im, im_mirror, cos_im, sin_im)):
            first = [jnp.where(top, cos_part[:8], plain[:8]), plain[8:]]
            pieces.append(jnp.concatenate(first + [jnp.where(top, sin_part[:8], mirror[:8]), mirror[8:]], axis=0))
        return pieces

    def columns_to_spectrum(i):
        for t in range(UNROLL):
            for odd in range(2):
                kz = i * (2 * UNROLL) + 2 * t + odd
                lines = [spec_ref[ri, pl.ds(kz, n, stride=ROWS), :] for ri in range(2)]
                freq_ref[t, odd, 0], freq_ref[t, odd, 1] = unfolded(dot(x_fwd_ref[...], folded(lines)), -1.0)

    def last_to_spectrum():
        freq_ref[0, 0, 0], freq_ref[0, 0, 1] = unfolded(dot(x_fwd_ref[...], folded([edge_ref[0], edge_ref[1]])), -1.0)
        freq_ref[0, 1] = jnp.zeros((2, n, w), f32)

    def spectrum_to_cross(holds_anchor, count=UNROLL):
        for t in range(count):
            re_a, im_a = freq_ref[t, 0, 0], freq_ref[t, 0, 1]
            re_b, im_b = freq_ref[t, 1, 0], freq_ref[t, 1, 1]
            re_one = jnp.where(lane < n, re_a, re_b)
            im_one = jnp.where(lane < n, im_a, im_b)
            re_two = swap(jnp.where(lane < n, re_b, re_a))
            im_two = swap(jnp.where(lane < n, im_b, im_a))
            cross_re = re_one * re_two + im_one * im_two
            cross_im = re_one * im_two - im_one * re_two
            power = cross_re * cross_re + cross_im * cross_im
            gain = lax.rsqrt(jnp.maximum(power, spectral_floor * spectral_floor))
            if holds_anchor and t == 0:
                gain = jnp.where(anchor, 0.0, gain)
            cross_re, cross_im = cross_re * gain, cross_im * (gain * exp_sign)
            cross_ref[t] = folded([cross_re, cross_im])

    def cross_to_wave(i, count=UNROLL):
        for t in range(count):
            at = i * UNROLL + t
            high, low = split(jnp.concatenate(unfolded(dot(x_fwd_ref[...], cross_ref[t]), 1.0), axis=1))
            wave_ref[0, pl.ds(pl.multiple_of(at * n, n), n), :] = high
            wave_ref[1, pl.ds(pl.multiple_of(at * n, n), n), :] = low

    def spectra(i, _):
        cross_to_wave(i - 2)
        spectrum_to_cross(False)
        columns_to_spectrum(i)
        return 0

    shift_copy.wait()
    for x in range(n):
        place_ref[x] = place(lax.rem(shift_ref[0, 1] + (n + x), n))
    columns_to_spectrum(0)
    spectrum_to_cross(True)
    columns_to_spectrum(1)
    lax.fori_loop(2, STEPS, spectra, 0)
    cross_to_wave(STEPS - 2)
    spectrum_to_cross(False)
    last_to_spectrum()
    cross_to_wave(STEPS - 1)
    spectrum_to_cross(False, 1)
    cross_to_wave(STEPS, 1)

    done = PLANES
    per = done // 2

    def inverse_y(i, _):
        at = pl.multiple_of(i * (per * n), per * n)
        high, low = wave_ref[0, pl.ds(at, per * n), :], wave_ref[1, pl.ds(at, per * n), :]
        lines = dot(jnp.concatenate([high, low, high], axis=1), yi_ref[...])
        for t in range(per):
            to = pl.multiple_of((i * per + t) * GAP, 8)
            line_ref[0, pl.ds(to, n), :] = lines[t * n : (t + 1) * n, :w]
            line_ref[1, pl.ds(to, n), :] = lines[t * n : (t + 1) * n, w:]
        return 0

    lax.fori_loop(0, 2, inverse_y, 0)

    lane = lax.broadcasted_iota(jnp.int32, (HALF, w), 1)
    x_per_step = 32
    x_per_copy = 8

    def planes(i, _):
        for t in range(x_per_step):
            pair = i * x_per_step + t
            cols = jnp.concatenate(
                [
                    jnp.concatenate([line_ref[ri, pl.ds(place_ref[2 * pair + p], GROUPS, stride=GAP), :] for ri in range(2)], axis=0)
                    for p in range(2)
                ],
                axis=1,
            )
            both = dot(zi_ref[...], three(cols))
            a_even, a_odd = both[:HALF, :w], both[:HALF, w:]
            b_even, b_odd = both[HALF:, :w], both[HALF:, w:]
            value = jnp.where(lane < n, a_even, b_odd) + swap(jnp.where(lane < n, a_odd, b_even))
            out_ref[:, pl.ds(pl.multiple_of(pair * w, w), w)] = value
            if t % x_per_copy == x_per_copy - 1:
                out_copy(i * (x_per_step // x_per_copy) + t // x_per_copy).start()
        return 0

    def out_copy(i):
        at = pl.ds(pl.multiple_of(i * (x_per_copy * w), x_per_copy * w), x_per_copy * w)
        return pltpu.make_async_copy(out_ref.at[:, at], out_hbm.at[:, at], out_sem.at[i])

    lax.fori_loop(0, HALF // x_per_step, planes, 0)
    for i in range(HALF // x_per_copy):
        out_copy(i).wait()


def share_tables(offsets, fractions):
    both = jnp.concatenate([offsets.astype(f32), fractions], axis=0)
    count = lax.axis_size("depth")
    slab = both.shape[1]
    lane = jnp.arange(2 * count * slab, dtype=jnp.int32) % (count * slab)
    mine = (lane // slab == lax.axis_index("depth")).astype(f32)
    table = jnp.tile(both, (1, 2 * count)) * mine
    step = count // 2
    while step > 2:
        table = table + lax.ppermute(table, "depth", [(i, i ^ step) for i in range(count)])
        step //= 2
    total = table
    for k in (1, 2, 3):
        total = total + lax.ppermute(table, "depth", [(i, i ^ k) for i in range(count)])
    return total


def windows(images, bricks_x, bricks_y):
    exps, tiles, depths = (lax.axis_size(a) for a in ("exp", "tile", "depth"))
    depth_index = lax.axis_index("depth")
    cams = images.shape[1]
    strip = lax.dynamic_slice_in_dim(images[0], depth_index % bricks_y * BRICK, BRICK, axis=2).reshape(cams, -1)

    def linear(e, t, d):
        return ((e % exps) * tiles + t % tiles) * depths + d

    def edge(step, other):
        edge_part = 0 if step == 1 else bricks_x - 1
        return [
            (linear(e, t, d), linear(e + other, t + step, d))
            for e in range(exps)
            for t in range(tiles)
            for d in range(depths)
            if d // bricks_y == edge_part
        ]

    axes = ("exp", "tile", "depth")
    tail = strip[:, -MARGIN * BRICK :]
    head = strip[:, : MARGIN * BRICK]
    pads = []
    for other in (0, 1):
        if bricks_x > 1:
            sent = jnp.where(depth_index // bricks_y == 0, tail, head)
            pads.append(lax.ppermute(sent, axes, edge(1, other) + edge(-1, other))[None])
        else:
            sides = ((tail, 1), (head, -1))
            pads.append(jnp.stack([lax.ppermute(v, axes, edge(step, other)) for v, step in sides]))
    piece = strip
    if bricks_x == 2:
        near = strip.shape[1] - MARGIN * BRICK
        piece = jnp.where(depth_index // bricks_y == 0, strip[:, :near], strip[:, -near:])
    other_strip = lax.ppermute(piece, "exp", [(i, (i + 1) % exps) for i in range(exps)])
    return strip, other_strip, pads[0], pads[1]


def per_device(images, offsets, fractions, shifts):
    cams, width, rows_y = images.shape[1:]
    bricks_x, bricks_y = width // BRICK, rows_y // BRICK
    assert cams == 4 and width % BRICK == 0 and rows_y % BRICK == 0
    assert bricks_x * bricks_y == lax.axis_size("depth")
    assert offsets.shape[1] * lax.axis_size("depth") == BRICK
    n = BRICK
    table = share_tables(offsets, fractions)
    strips = windows(images, bricks_x, bricks_y)
    window = (n + 2 * MARGIN) * n
    extended = (width + 2 * MARGIN) * n
    vmem = pl.BlockSpec(memory_space=pltpu.VMEM)
    z_fwd, y_fwd, x_fwd, *inverses = (jnp.asarray(v) for v in constant_tables())
    turned = pl.pallas_call(
        turn,
        out_shape=[
            jax.ShapeDtypeStruct((12 * n, 4 * n), bf16),
            jax.ShapeDtypeStruct((n, 6 * GROUPS), bf16),
        ],
        in_specs=[pl.BlockSpec(memory_space=pltpu.SMEM)] + [vmem] * 2,
        out_specs=[vmem] * 2,
        compiler_params=pltpu.CompilerParams(vmem_limit_bytes=8 * 1024 * 1024),
    )(shifts, *inverses)
    ready = pl.pallas_call(
        functools.partial(prepare, bricks_y=bricks_y),
        out_shape=[
            jax.ShapeDtypeStruct((8, 2 * window), f32),
            jax.ShapeDtypeStruct((16, 2 * window), bf16),
            jax.ShapeDtypeStruct((16, 2 * window), bf16),
        ],
        in_specs=[vmem] * 4,
        out_specs=[vmem] * 3,
        scratch_shapes=[pltpu.VMEM((8, extended), f32)],
        compiler_params=pltpu.CompilerParams(vmem_limit_bytes=16 * 1024 * 1024),
    )(*strips)
    second = (n + 18) * 2 * n
    out = pl.pallas_call(
        kernel,
        out_shape=jax.ShapeDtypeStruct((HALF, n * n), f32),
        in_specs=[pl.BlockSpec(memory_space=pl.ANY)] + [vmem] * 9,
        out_specs=pl.BlockSpec(memory_space=pl.ANY),
        scratch_shapes=[
            pltpu.VMEM((16, second), bf16),
            pltpu.VMEM((16, second), bf16),
            pltpu.VMEM((8 * PAIRS, (n + 2 * REACH) * 2 * n), f32),
            pltpu.VMEM((2, n * ROWS, 2 * n), f32),
            pltpu.VMEM((2, n, 2 * n), f32),
            pltpu.VMEM((UNROLL, 2, 2, n, 2 * n), f32),
            pltpu.VMEM((UNROLL, 3 * n, 4 * n), bf16),
            pltpu.VMEM((2, PLANES * n, 4 * n), bf16),
            pltpu.VMEM((2, GROUPS * GAP, 2 * n), f32),
            pltpu.VMEM((n, 224), bf16),
            pltpu.VMEM((8 * PAIRS, 3 * n), bf16),
            pltpu.VMEM((HALF, n * n), f32),
            pltpu.SemaphoreType.DMA((4,)),
            pltpu.SMEM(shifts.shape, jnp.int32),
            pltpu.SemaphoreType.DMA(()),
            pltpu.SMEM((n,), jnp.int32),
        ],
        compiler_params=pltpu.CompilerParams(vmem_limit_bytes=40 * 1024 * 1024),
    )(shifts, table, *ready, *turned, z_fwd, y_fwd, x_fwd)
    return out.reshape(1, HALF, n * n)


def solution(mesh):
    placed = (
        P("exp", None, "tile", None),
        P(None, "depth"),
        P(None, "depth"),
        P(("tile", "depth"), None),
    )
    return jax.shard_map(
        per_device,
        mesh=mesh,
        in_specs=placed,
        out_specs=P(("tile", "depth"), "exp", None),
        check_vma=False,
    )
```

```python
import functools
import math

import jax
import jax.numpy as jnp
import numpy as np
from jax import lax
from jax.experimental import pallas as pl
from jax.experimental.pallas import tpu as pltpu
from jax.sharding import PartitionSpec as P


BRICK = 64
HALF = BRICK // 2
ROWS = 40
MARGIN = 32
SHIFT_LOW = -8
PAIRS = 9
REACH = 18
UNROLL = 2
STEPS = 8
PLANES = 18
GROUPS = 24
GAP = 72
spectral_floor = 0.01
f32, bf16 = jnp.float32, jnp.bfloat16


def split(value):
    high = value.astype(bf16)
    return high, (value - high.astype(f32)).astype(bf16)


def dot(a, b):
    return jnp.dot(a, b, preferred_element_type=f32)


def tent_value(distance, fraction):
    return jnp.maximum(0.0, 1.0 - jnp.abs(distance - fraction) / 1.5)


def dft_parts():
    wave = np.arange(BRICK)
    angle = (wave[:, None] * wave[None, :] % BRICK) * (2.0 * math.pi / BRICK)
    return np.cos(angle) / math.sqrt(BRICK), np.sin(angle) / math.sqrt(BRICK)


def host_split(value):
    high = value.astype(np.float32).astype(bf16)
    return high, (value - high.astype(np.float64)).astype(np.float32).astype(bf16)


def constant_tables():
    c, s = dft_parts()
    n = BRICK
    high, low = host_split(np.concatenate([c[: HALF + 1], -s[1:HALF]], axis=0))
    z_fwd = np.concatenate([high, high, low], axis=1)
    yt = np.zeros((2, 2, n, 2, 2, n))
    for e in range(2):
        yt[0, e, :, 0, e], yt[0, e, :, 1, e] = c, -s
        yt[1, e, :, 0, e], yt[1, e, :, 1, e] = s, c
    high, low = host_split(yt.reshape(4 * n, 4 * n))
    y_fwd = np.concatenate([high, high, low], axis=0)
    fold = np.zeros((n, n))
    fold[:HALF, 1:HALF], fold[HALF, 1:HALF] = c[:HALF, 1:HALF], c[HALF, 1:HALF]
    fold[HALF + 1 :, HALF + 1 :] = s[1:HALF, 1:HALF]
    fold[0 : HALF + 1 : 2, 0] = fold[1:HALF:2, HALF] = c[0, 0]
    high, low = host_split(fold)
    x_fwd = np.concatenate([high, high, low], axis=1)
    twice = lambda t: np.concatenate([t, t], axis=0)
    y_inv = np.stack([np.concatenate([twice(c), twice(-s)], 1).T, np.concatenate([twice(s), twice(c)], 1).T])
    y_inv = y_inv.astype(np.float32)
    weight = np.zeros(2 * GROUPS)
    weight[: HALF + 1] = 2.0
    weight[0] = weight[HALF] = 1.0
    z_inv = []
    for odd in range(2):
        pick = np.concatenate([(t[:, : 2 * GROUPS] * weight)[:, odd::2] for t in (c, -s)], axis=1)
        whole = twice(np.pad(np.tile(pick, (1, 3)), ((0, 0), (0, 4 * n - 6 * GROUPS))))
        z_inv.append(np.stack([whole[:, : 2 * n], whole[:, 2 * n :]]))
    return z_fwd, y_fwd, x_fwd, y_inv, np.stack(z_inv).astype(np.float32)


def pack(both, pack_ref, high_ref):
    w = 2 * BRICK
    high = both.astype(bf16).astype(f32)
    pack_ref[...] = jnp.concatenate([high, both - high], axis=0).astype(bf16)
    later = jnp.concatenate([high[:, 2 * w :], high[:, : 2 * w]], axis=1)
    high_ref[...] = jnp.concatenate([high, later], axis=0).astype(bf16)


def turn(shift_ref, y_inv_ref, z_inv_ref, yi_ref, zi_ref):
    n = BRICK
    w = 2 * n
    exp_index = lax.axis_index("exp")

    sz, sy = shift_ref[0, 0] + n, shift_ref[0, 2] + n
    lane = lax.broadcasted_iota(jnp.int32, (n, w), 1)
    back = lax.rem(w - lax.rem(sy, n), w)
    for ri_out in range(2):
        turned = pltpu.roll(y_inv_ref[ri_out], back, 1)
        pieces = []
        for ri in range(2):
            piece = turned[ri * n : (ri + 1) * n]
            pieces += [jnp.where(lane < n, piece, 0.0), jnp.where(lane < n, 0.0, piece)]
        high, low = split(jnp.concatenate(pieces, axis=0))
        at = slice(ri_out * w, (ri_out + 1) * w)
        yi_ref[0 : 2 * w, at] = high
        yi_ref[2 * w : 4 * w, at] = high
        yi_ref[4 * w :, at] = low
    first = lax.rem(HALF * exp_index + sz, n)
    turned = [jnp.concatenate([z_inv_ref[p, h, pl.ds(first, HALF), :] for h in range(2)], axis=1) for p in range(2)]
    turned = jnp.concatenate(turned, axis=0)
    high, low = split(turned)
    col = lax.broadcasted_iota(jnp.int32, turned.shape, 1)
    zi_ref[...] = jnp.where(col < 4 * GROUPS, high.astype(f32), low.astype(f32)).astype(bf16)[:, : 6 * GROUPS]


def prepare(
    own_ref, other_ref, pad_own_ref, pad_other_ref, first_ref, pack_ref, high_ref, raw_ref,
    *, bricks_y,
):
    n = BRICK
    w = 2 * n
    part = lax.axis_index("depth") // bricks_y
    columns = n + 2 * MARGIN
    pad = MARGIN * n
    strip = own_ref.shape[1]

    raw_ref[0:4, 0:pad] = pad_own_ref[0]
    raw_ref[4:8, 0:pad] = pad_other_ref[0]
    raw_ref[0:4, pad : pad + strip] = own_ref[...]
    reach = other_ref.shape[1]
    at = pad + part * (strip - reach) if reach < strip else pad
    raw_ref[4:8, pl.ds(pl.multiple_of(at, pad), reach)] = other_ref[...]
    raw_ref[0:4, pad + strip :] = pad_own_ref[pad_own_ref.shape[0] - 1]
    raw_ref[4:8, pad + strip :] = pad_other_ref[pad_other_ref.shape[0] - 1]
    row = lax.broadcasted_iota(jnp.int32, (8, w), 0)
    lane = lax.broadcasted_iota(jnp.int32, (8, w), 1)
    same = (row < 4) == (lane < n)
    swap = lambda v: pltpu.roll(v, n, 1)
    ratio = jnp.log(raw_ref[:, pl.ds(pl.multiple_of(part * (n * n), n * n), columns * n)])
    even, odd = [], []
    for k in range(columns // 2):
        here = ratio[:, k * w : (k + 1) * w]
        flipped = pltpu.roll(here, 4, 0)
        even.append(jnp.where(same, here, swap(flipped)))
        odd.append(jnp.where(same, swap(here), flipped))
    cols = []
    for k in range(columns // 2):
        cols += [even[k], jnp.where(row < 4, odd[k], odd[(k + 1) % (columns // 2)])]
    cols = jnp.concatenate(cols, axis=1)
    first_ref[...] = cols
    pack(cols, pack_ref, high_ref)


def kernel(
    shift_any, tab_ref, first_ref, pack_in_ref, high_in_ref, yi_ref, zi_ref, z_fwd_ref, y_fwd_ref, x_fwd_ref,
    out_hbm,
    pack_ref, high_ref, shifted_ref, spec_ref, edge_ref, freq_ref, cross_ref,
    wave_ref, line_ref, back_ref, forward_ref,
    out_ref, out_sem, shift_ref, shift_sem, place_ref,
):
    n = BRICK
    w = 2 * n
    exp_index = lax.axis_index("exp")

    shift_copy = pltpu.make_async_copy(shift_any, shift_ref, shift_sem)
    shift_copy.start()
    line_ref[:, PLANES * GAP :, :] = jnp.zeros((2, (GROUPS - PLANES) * GAP, w), f32)
    wave_ref[:, (PLANES - 1) * n :, :] = jnp.zeros((2, n, 2 * w), bf16)

    tab = tab_ref[...]
    rows = lax.broadcasted_iota(jnp.int32, (8, w), 0)
    offs = jnp.where(rows < 4, tab, pltpu.roll(tab, 4, 0))
    frac = jnp.where(rows < 4, pltpu.roll(tab, 4, 0), tab)
    total = sum(tent_value(float(d), frac) for d in range(-2, 4))
    parity = (rows >= 4).astype(f32)
    blocks = [tent_value(SHIFT_LOW + 2 * q + parity - offs, frac) / total for q in range(PAIRS)]
    sums = jnp.sum(sum(blocks)[:, :n], axis=1, keepdims=True) / n
    uniform = jnp.log(sums + pltpu.roll(jnp.broadcast_to(sums, (8, w)), 4, 0)[:, :1])
    faint = jnp.exp(-jnp.sum(sum(blocks) * uniform, axis=0, keepdims=True) / 4.0)
    both_high, back_low = [], []
    for block in blocks:
        high, low = split(block / 4.0)
        both_high += [high.astype(f32)] * 2
        back_low.append(low.astype(f32))
    stacked = jnp.concatenate(both_high + back_low + [jnp.zeros((40, w), f32)], axis=0)
    back_ref[...] = jnp.transpose(stacked)[:n, :224].astype(bf16)
    high, low = split(jnp.concatenate(blocks, axis=0) * (faint / n))
    forward_ref[...] = jnp.concatenate([high, low], axis=1)[:, : 3 * n]

    swap = lambda v: pltpu.roll(v, n, 1)

    def spread(pack_from, high_from, first_lane, count):
        pieces = [pack_from[:, pl.ds(first_lane + 2 * w * q, count)] for q in range(PAIRS)]
        pieces += [high_from[:, pl.ds(first_lane + 2 * w * q, count)] for q in range(0, PAIRS, 2)]
        return jnp.concatenate(pieces, axis=0)

    lo_x, hi_x = -REACH, n + REACH
    chunk = 100 * w
    back_w = back_ref[...]
    forward_w = forward_ref[...]

    def first_pass(i, _):
        start = pl.multiple_of(i * chunk, 2 * w)
        logv = dot(back_w, spread(pack_in_ref, high_in_ref, start + (lo_x + SHIFT_LOW + MARGIN) * w, chunk))
        high, low = split(jnp.exp(logv))
        shifted_ref[:, pl.ds(start, chunk)] = dot(forward_w, jnp.concatenate([high, low, high], axis=0))
        return 0

    lax.fori_loop(0, (hi_x - lo_x) * w // chunk, first_pass, 0)

    lo_u, hi_u = -10, n + 10
    count = (hi_u - lo_u) * w
    gathered = sum(
        shifted_ref[8 * q : 8 * q + 8, pl.ds((lo_u - SHIFT_LOW - 2 * q - lo_x) * w, count)] for q in range(PAIRS)
    )
    proj = gathered[:, 2 * w :] + pltpu.roll(gathered[:, w : count - w], 4, 0)
    ratio = first_ref[:, (lo_u + 2 + MARGIN) * w : (hi_u + MARGIN) * w]
    ratio = (ratio - uniform) + (ratio - jnp.log(proj))
    later = pltpu.roll(jnp.concatenate([ratio[:, w:], ratio[:, :w]], axis=1), 4, 0)
    pack(jnp.where(lax.broadcasted_iota(jnp.int32, ratio.shape, 0) < 4, ratio, later), pack_ref, high_ref)

    top = lax.broadcasted_iota(jnp.int32, (8, w), 0) == 0
    place = lambda x: jnp.where(x <= HALF, x, n + HALF - x)

    per = 64
    chunk2 = per * w

    def second_pass(i, _):
        start = pl.multiple_of(i * chunk2, chunk2)
        logv = dot(back_w, spread(pack_ref, high_ref, start, chunk2))
        high, low = split(jnp.exp(logv))
        spec = dot(z_fwd_ref[...], jnp.concatenate([high, low, high], axis=0))
        groups = []
        for j in range(per):
            piece = spec[:, w * j : w * (j + 1)]
            imag = jnp.concatenate([jnp.where(top, 0.0, piece[HALF : HALF + 8]), piece[HALF + 8 :]], axis=0)
            groups.append(jnp.concatenate([piece[:HALF], imag], axis=1))
            edge_ref[0, pl.ds(place(i * per + j), 1), :] = piece[HALF : HALF + 1]
        high, low = split(jnp.concatenate(groups, axis=0))
        lines = dot(jnp.concatenate([high, low, high], axis=1), y_fwd_ref[...])
        for j in range(per):
            at = pl.multiple_of(place(i * per + j) * ROWS, ROWS)
            spec_ref[0, pl.ds(at, HALF), :] = lines[j * HALF : (j + 1) * HALF, :w]
            spec_ref[1, pl.ds(at, HALF), :] = lines[j * HALF : (j + 1) * HALF, w:]
        return 0

    lax.fori_loop(0, n // per, second_pass, 0)
    high, low = split(jnp.concatenate([edge_ref[0], jnp.zeros((n, w), f32)], axis=1))
    lines = dot(jnp.concatenate([high, low, high], axis=1), y_fwd_ref[...])
    edge_ref[0], edge_ref[1] = lines[:, :w], lines[:, w:]

    lane = lax.broadcasted_iota(jnp.int32, (n, w), 1)
    row = lax.broadcasted_iota(jnp.int32, (n, w), 0)
    own_sign = jnp.where(exp_index == 0, 1.0, -1.0)
    exp_sign = jnp.where(lane < n, own_sign, -own_sign)
    anchor = (lane == 0) & (row == 0)

    def three(value):
        high, low = split(value)
        return jnp.concatenate([high, low, high], axis=0)

    def folded(pieces):
        value = jnp.concatenate(pieces, axis=1)
        return three(jnp.concatenate([value[:HALF] + value[HALF:], value[:HALF] - value[HALF:]], axis=0))

    def unfolded(both, sign):
        cos_re, cos_im, sin_re, sin_im = (both[r : r + HALF, c : c + w] for r in (0, HALF) for c in (0, w))
        re, re_mirror = cos_re - sin_im, cos_re + sin_im
        im, im_mirror = cos_im + sin_re, cos_im - sin_re
        if sign < 0:
            re, re_mirror, im, im_mirror = re_mirror, re, im_mirror, im
        pieces = []
        for plain, mirror, cos_part, sin_part in ((re, re_mirror, cos_re, sin_re), (im, im_mirror, cos_im, sin_im)):
            first = [jnp.where(top, cos_part[:8], plain[:8]), plain[8:]]
            pieces.append(jnp.concatenate(first + [jnp.where(top, sin_part[:8], mirror[:8]), mirror[8:]], axis=0))
        return pieces

    def columns_to_spectrum(i):
        for t in range(UNROLL):
            for odd in range(2):
                kz = i * (2 * UNROLL) + 2 * t + odd
                lines = [spec_ref[ri, pl.ds(kz, n, stride=ROWS), :] for ri in range(2)]
                freq_ref[t, odd, 0], freq_ref[t, odd, 1] = unfolded(dot(x_fwd_ref[...], folded(lines)), -1.0)

    def last_to_spectrum():
        freq_ref[0, 0, 0], freq_ref[0, 0, 1] = unfolded(dot(x_fwd_ref[...], folded([edge_ref[0], edge_ref[1]])), -1.0)
        freq_ref[0, 1] = jnp.zeros((2, n, w), f32)

    def spectrum_to_cross(holds_anchor, count=UNROLL):
        for t in range(count):
            re_a, im_a = freq_ref[t, 0, 0], freq_ref[t, 0, 1]
            re_b, im_b = freq_ref[t, 1, 0], freq_ref[t, 1, 1]
            re_one = jnp.where(lane < n, re_a, re_b)
            im_one = jnp.where(lane < n, im_a, im_b)
            re_two = swap(jnp.where(lane < n, re_b, re_a))
            im_two = swap(jnp.where(lane < n, im_b, im_a))
            cross_re = re_one * re_two + im_one * im_two
            cross_im = re_one * im_two - im_one * re_two
            power = cross_re * cross_re + cross_im * cross_im
            gain = lax.rsqrt(jnp.maximum(power, spectral_floor * spectral_floor))
            if holds_anchor and t == 0:
                gain = jnp.where(anchor, 0.0, gain)
            cross_re, cross_im = cross_re * gain, cross_im * (gain * exp_sign)
            cross_ref[t] = folded([cross_re, cross_im])

    def cross_to_wave(i, count=UNROLL):
        for t in range(count):
            at = i * UNROLL + t
            high, low = split(jnp.concatenate(unfolded(dot(x_fwd_ref[...], cross_ref[t]), 1.0), axis=1))
            wave_ref[0, pl.ds(pl.multiple_of(at * n, n), n), :] = high
            wave_ref[1, pl.ds(pl.multiple_of(at * n, n), n), :] = low

    def spectra(i, _):
        cross_to_wave(i - 2)
        spectrum_to_cross(False)
        columns_to_spectrum(i)
        return 0

    shift_copy.wait()
    for x in range(n):
        place_ref[x] = place(lax.rem(shift_ref[0, 1] + (n + x), n))
    columns_to_spectrum(0)
    spectrum_to_cross(True)
    columns_to_spectrum(1)
    lax.fori_loop(2, STEPS, spectra, 0)
    cross_to_wave(STEPS - 2)
    spectrum_to_cross(False)
    last_to_spectrum()
    cross_to_wave(STEPS - 1)
    spectrum_to_cross(False, 1)
    cross_to_wave(STEPS, 1)

    done = PLANES
    per = done // 2

    def inverse_y(i, _):
        at = pl.multiple_of(i * (per * n), per * n)
        high, low = wave_ref[0, pl.ds(at, per * n), :], wave_ref[1, pl.ds(at, per * n), :]
        lines = dot(jnp.concatenate([high, low, high], axis=1), yi_ref[...])
        for t in range(per):
            to = pl.multiple_of((i * per + t) * GAP, 8)
            line_ref[0, pl.ds(to, n), :] = lines[t * n : (t + 1) * n, :w]
            line_ref[1, pl.ds(to, n), :] = lines[t * n : (t + 1) * n, w:]
        return 0

    lax.fori_loop(0, 2, inverse_y, 0)

    lane = lax.broadcasted_iota(jnp.int32, (HALF, w), 1)
    x_per_step = 32
    x_per_copy = 8

    def planes(i, _):
        for t in range(x_per_step):
            pair = i * x_per_step + t
            cols = jnp.concatenate(
                [
                    jnp.concatenate([line_ref[ri, pl.ds(place_ref[2 * pair + p], GROUPS, stride=GAP), :] for ri in range(2)], axis=0)
                    for p in range(2)
                ],
                axis=1,
            )
            both = dot(zi_ref[...], three(cols))
            a_even, a_odd = both[:HALF, :w], both[:HALF, w:]
            b_even, b_odd = both[HALF:, :w], both[HALF:, w:]
            value = jnp.where(lane < n, a_even, b_odd) + swap(jnp.where(lane < n, a_odd, b_even))
            out_ref[:, pl.ds(pl.multiple_of(pair * w, w), w)] = value
            if t % x_per_copy == x_per_copy - 1:
                out_copy(i * (x_per_step // x_per_copy) + t // x_per_copy).start()
        return 0

    def out_copy(i):
        at = pl.ds(pl.multiple_of(i * (x_per_copy * w), x_per_copy * w), x_per_copy * w)
        return pltpu.make_async_copy(out_ref.at[:, at], out_hbm.at[:, at], out_sem.at[i])

    lax.fori_loop(0, HALF // x_per_step, planes, 0)
    for i in range(HALF // x_per_copy):
        out_copy(i).wait()


def share_tables(offsets, fractions):
    both = jnp.concatenate([offsets.astype(f32), fractions], axis=0)
    count = lax.axis_size("depth")
    slab = both.shape[1]
    lane = jnp.arange(2 * count * slab, dtype=jnp.int32) % (count * slab)
    mine = (lane // slab == lax.axis_index("depth")).astype(f32)
    table = jnp.tile(both, (1, 2 * count)) * mine
    total = table
    for k in (1, 2, 3):
        total = total + lax.ppermute(table, "depth", [(i, i ^ k) for i in range(count)])
    table = total
    step = 4
    while step < count:
        table = table + lax.ppermute(table, "depth", [(i, i ^ step) for i in range(count)])
        step *= 2
    return table


def windows(images, bricks_x, bricks_y):
    exps, tiles, depths = (lax.axis_size(a) for a in ("exp", "tile", "depth"))
    depth_index = lax.axis_index("depth")
    cams = images.shape[1]
    strip = lax.dynamic_slice_in_dim(images[0], depth_index % bricks_y * BRICK, BRICK, axis=2).reshape(cams, -1)

    def linear(e, t, d):
        return ((e % exps) * tiles + t % tiles) * depths + d

    def edge(step, other):
        edge_part = 0 if step == 1 else bricks_x - 1
        return [
            (linear(e, t, d), linear(e + other, t + step, d))
            for e in range(exps)
            for t in range(tiles)
            for d in range(depths)
            if d // bricks_y == edge_part
        ]

    axes = ("exp", "tile", "depth")
    tail = strip[:, -MARGIN * BRICK :]
    head = strip[:, : MARGIN * BRICK]
    pads = []
    for other in (0, 1):
        if bricks_x > 1:
            sent = jnp.where(depth_index // bricks_y == 0, tail, head)
            pads.append(lax.ppermute(sent, axes, edge(1, other) + edge(-1, other))[None])
        else:
            sides = ((tail, 1), (head, -1))
            pads.append(jnp.stack([lax.ppermute(v, axes, edge(step, other)) for v, step in sides]))
    piece = strip
    if bricks_x == 2:
        near = strip.shape[1] - MARGIN * BRICK
        piece = jnp.where(depth_index // bricks_y == 0, strip[:, :near], strip[:, -near:])
    other_strip = lax.ppermute(piece, "exp", [(i, (i + 1) % exps) for i in range(exps)])
    return strip, other_strip, pads[0], pads[1]


def per_device(images, offsets, fractions, shifts):
    cams, width, rows_y = images.shape[1:]
    bricks_x, bricks_y = width // BRICK, rows_y // BRICK
    assert cams == 4 and width % BRICK == 0 and rows_y % BRICK == 0
    assert bricks_x * bricks_y == lax.axis_size("depth")
    assert offsets.shape[1] * lax.axis_size("depth") == BRICK
    n = BRICK
    table = share_tables(offsets, fractions)
    strips = windows(images, bricks_x, bricks_y)
    window = (n + 2 * MARGIN) * n
    extended = (width + 2 * MARGIN) * n
    vmem = pl.BlockSpec(memory_space=pltpu.VMEM)
    z_fwd, y_fwd, x_fwd, *inverses = (jnp.asarray(v) for v in constant_tables())
    turned = pl.pallas_call(
        turn,
        out_shape=[
            jax.ShapeDtypeStruct((12 * n, 4 * n), bf16),
            jax.ShapeDtypeStruct((n, 6 * GROUPS), bf16),
        ],
        in_specs=[pl.BlockSpec(memory_space=pltpu.SMEM)] + [vmem] * 2,
        out_specs=[vmem] * 2,
        compiler_params=pltpu.CompilerParams(vmem_limit_bytes=8 * 1024 * 1024),
    )(shifts, *inverses)
    ready = pl.pallas_call(
        functools.partial(prepare, bricks_y=bricks_y),
        out_shape=[
            jax.ShapeDtypeStruct((8, 2 * window), f32),
            jax.ShapeDtypeStruct((16, 2 * window), bf16),
            jax.ShapeDtypeStruct((16, 2 * window), bf16),
        ],
        in_specs=[vmem] * 4,
        out_specs=[vmem] * 3,
        scratch_shapes=[pltpu.VMEM((8, extended), f32)],
        compiler_params=pltpu.CompilerParams(vmem_limit_bytes=16 * 1024 * 1024),
    )(*strips)
    second = (n + 18) * 2 * n
    out = pl.pallas_call(
        kernel,
        out_shape=jax.ShapeDtypeStruct((HALF, n * n), f32),
        in_specs=[pl.BlockSpec(memory_space=pl.ANY)] + [vmem] * 9,
        out_specs=pl.BlockSpec(memory_space=pl.ANY),
        scratch_shapes=[
            pltpu.VMEM((16, second), bf16),
            pltpu.VMEM((16, second), bf16),
            pltpu.VMEM((8 * PAIRS, (n + 2 * REACH) * 2 * n), f32),
            pltpu.VMEM((2, n * ROWS, 2 * n), f32),
            pltpu.VMEM((2, n, 2 * n), f32),
            pltpu.VMEM((UNROLL, 2, 2, n, 2 * n), f32),
            pltpu.VMEM((UNROLL, 3 * n, 4 * n), bf16),
            pltpu.VMEM((2, PLANES * n, 4 * n), bf16),
            pltpu.VMEM((2, GROUPS * GAP, 2 * n), f32),
            pltpu.VMEM((n, 224), bf16),
            pltpu.VMEM((8 * PAIRS, 3 * n), bf16),
            pltpu.VMEM((HALF, n * n), f32),
            pltpu.SemaphoreType.DMA((4,)),
            pltpu.SMEM(shifts.shape, jnp.int32),
            pltpu.SemaphoreType.DMA(()),
            pltpu.SMEM((n,), jnp.int32),
        ],
        compiler_params=pltpu.CompilerParams(vmem_limit_bytes=40 * 1024 * 1024),
    )(shifts, table, *ready, *turned, z_fwd, y_fwd, x_fwd)
    return out.reshape(1, HALF, n * n)


def solution(mesh):
    placed = (
        P("exp", None, "tile", None),
        P(None, "depth"),
        P(None, "depth"),
        P(("tile", "depth"), None),
    )
    return jax.shard_map(
        per_device,
        mesh=mesh,
        in_specs=placed,
        out_specs=P(("tile", "depth"), "exp", None),
        check_vma=False,
    )
```

```python
import functools
import math

import jax
import jax.numpy as jnp
import numpy as np
from jax import lax
from jax.experimental import pallas as pl
from jax.experimental.pallas import tpu as pltpu
from jax.sharding import PartitionSpec as P


BRICK = 64
HALF = BRICK // 2
ROWS = 40
MARGIN = 26
SHIFT_LOW = -8
PAIRS = 9
REACH = 18
UNROLL = 2
STEPS = 8
PLANES = 17
GROUPS = 24
GAP = 72
spectral_floor = 0.01
f32, bf16 = jnp.float32, jnp.bfloat16


def split(value):
    high = value.astype(bf16)
    return high, (value - high.astype(f32)).astype(bf16)


def dot(a, b):
    return jnp.dot(a, b, preferred_element_type=f32)


def tent_value(distance, fraction):
    return jnp.maximum(0.0, 1.0 - jnp.abs(distance - fraction) / 1.5)


def dft_parts():
    wave = np.arange(BRICK)
    angle = (wave[:, None] * wave[None, :] % BRICK) * (2.0 * math.pi / BRICK)
    return np.cos(angle) / math.sqrt(BRICK), np.sin(angle) / math.sqrt(BRICK)


def host_split(value):
    high = value.astype(np.float32).astype(bf16)
    return high, (value - high.astype(np.float64)).astype(np.float32).astype(bf16)


def constant_tables():
    c, s = dft_parts()
    n = BRICK
    high, low = host_split(np.concatenate([c[: HALF + 1], -s[1:HALF]], axis=0))
    z_fwd = np.concatenate([high, high, low], axis=1)
    yt = np.zeros((2, 2, n, 2, 2, n))
    for e in range(2):
        yt[0, e, :, 0, e], yt[0, e, :, 1, e] = c, -s
        yt[1, e, :, 0, e], yt[1, e, :, 1, e] = s, c
    high, low = host_split(yt.reshape(4 * n, 4 * n))
    y_fwd = np.concatenate([high, high, low], axis=0)
    fold = np.zeros((n, n))
    fold[:HALF, 1:HALF], fold[HALF, 1:HALF] = c[:HALF, 1:HALF], c[HALF, 1:HALF]
    fold[HALF + 1 :, HALF + 1 :] = s[1:HALF, 1:HALF]
    fold[0 : HALF + 1 : 2, 0] = fold[1:HALF:2, HALF] = c[0, 0]
    high, low = host_split(fold)
    x_fwd = np.concatenate([high, high, low], axis=1)
    twice = lambda t: np.concatenate([t, t], axis=0)
    y_inv = np.stack([np.concatenate([twice(c), twice(-s)], 1).T, np.concatenate([twice(s), twice(c)], 1).T])
    y_inv = y_inv.astype(np.float32)
    weight = np.zeros(2 * GROUPS)
    weight[: HALF + 1] = 2.0
    weight[0] = weight[HALF] = 1.0
    z_inv = []
    for odd in range(2):
        pick = np.concatenate([(t[:, : 2 * GROUPS] * weight)[:, odd::2] for t in (c, -s)], axis=1)
        whole = twice(np.pad(np.tile(pick, (1, 3)), ((0, 0), (0, 4 * n - 6 * GROUPS))))
        z_inv.append(np.stack([whole[:, : 2 * n], whole[:, 2 * n :]]))
    return z_fwd, y_fwd, x_fwd, y_inv, np.stack(z_inv).astype(np.float32)


def pack(both, pack_ref, high_ref):
    w = 2 * BRICK
    high = both.astype(bf16).astype(f32)
    pack_ref[...] = jnp.concatenate([high, both - high], axis=0).astype(bf16)
    later = jnp.concatenate([high[:, 2 * w :], high[:, : 2 * w]], axis=1)
    high_ref[...] = jnp.concatenate([high, later], axis=0).astype(bf16)


def turn(shift_ref, y_inv_ref, z_inv_ref, yi_ref, zi_ref):
    n = BRICK
    w = 2 * n
    exp_index = lax.axis_index("exp")

    sz, sy = shift_ref[0, 0] + n, shift_ref[0, 2] + n
    lane = lax.broadcasted_iota(jnp.int32, (n, w), 1)
    back = lax.rem(w - lax.rem(sy, n), w)
    for ri_out in range(2):
        turned = pltpu.roll(y_inv_ref[ri_out], back, 1)
        pieces = []
        for ri in range(2):
            piece = turned[ri * n : (ri + 1) * n]
            pieces += [jnp.where(lane < n, piece, 0.0), jnp.where(lane < n, 0.0, piece)]
        high, low = split(jnp.concatenate(pieces, axis=0))
        at = slice(ri_out * w, (ri_out + 1) * w)
        yi_ref[0 : 2 * w, at] = high
        yi_ref[2 * w : 4 * w, at] = high
        yi_ref[4 * w :, at] = low
    first = lax.rem(HALF * exp_index + sz, n)
    turned = [jnp.concatenate([z_inv_ref[p, h, pl.ds(first, HALF), :] for h in range(2)], axis=1) for p in range(2)]
    turned = jnp.concatenate(turned, axis=0)
    high, low = split(turned)
    col = lax.broadcasted_iota(jnp.int32, turned.shape, 1)
    zi_ref[...] = jnp.where(col < 4 * GROUPS, high.astype(f32), low.astype(f32)).astype(bf16)[:, : 6 * GROUPS]


def prepare(
    own_ref, other_ref, pad_own_ref, pad_other_ref, first_ref, pack_ref, high_ref, raw_ref,
    *, bricks_y,
):
    n = BRICK
    w = 2 * n
    part = lax.axis_index("depth") // bricks_y
    columns = n + 2 * MARGIN
    pad = MARGIN * n
    strip = own_ref.shape[1]

    raw_ref[0:4, 0:pad] = pad_own_ref[0]
    raw_ref[4:8, 0:pad] = pad_other_ref[0]
    raw_ref[0:4, pad : pad + strip] = own_ref[...]
    reach = other_ref.shape[1]
    at = pad + part * (strip - reach) if reach < strip else pad
    raw_ref[4:8, pl.ds(pl.multiple_of(at, pad), reach)] = other_ref[...]
    raw_ref[0:4, pad + strip :] = pad_own_ref[pad_own_ref.shape[0] - 1]
    raw_ref[4:8, pad + strip :] = pad_other_ref[pad_other_ref.shape[0] - 1]
    row = lax.broadcasted_iota(jnp.int32, (8, w), 0)
    lane = lax.broadcasted_iota(jnp.int32, (8, w), 1)
    same = (row < 4) == (lane < n)
    swap = lambda v: pltpu.roll(v, n, 1)
    ratio = jnp.log(raw_ref[:, pl.ds(pl.multiple_of(part * (n * n), n * n), columns * n)])
    even, odd = [], []
    for k in range(columns // 2):
        here = ratio[:, k * w : (k + 1) * w]
        flipped = pltpu.roll(here, 4, 0)
        even.append(jnp.where(same, here, swap(flipped)))
        odd.append(jnp.where(same, swap(here), flipped))
    cols = []
    for k in range(columns // 2):
        cols += [even[k], jnp.where(row < 4, odd[k], odd[(k + 1) % (columns // 2)])]
    cols = jnp.concatenate(cols, axis=1)
    first_ref[...] = cols
    pack(cols, pack_ref, high_ref)


def kernel(
    shift_any, tab_ref, first_ref, pack_in_ref, high_in_ref, yi_ref, zi_ref, z_fwd_ref, y_fwd_ref, x_fwd_ref,
    out_hbm,
    pack_ref, high_ref, shifted_ref, spec_ref, edge_ref, freq_ref, cross_ref,
    wave_ref, line_ref, back_ref, forward_ref,
    out_ref, out_sem, shift_ref, shift_sem, place_ref,
):
    n = BRICK
    w = 2 * n
    exp_index = lax.axis_index("exp")

    shift_copy = pltpu.make_async_copy(shift_any, shift_ref, shift_sem)
    shift_copy.start()
    line_ref[:, PLANES * GAP :, :] = jnp.zeros((2, (GROUPS - PLANES) * GAP, w), f32)

    tab = tab_ref[...]
    rows = lax.broadcasted_iota(jnp.int32, (8, w), 0)
    offs = jnp.where(rows < 4, tab, pltpu.roll(tab, 4, 0))
    frac = jnp.where(rows < 4, pltpu.roll(tab, 4, 0), tab)
    total = sum(tent_value(float(d), frac) for d in range(-2, 4))
    parity = (rows >= 4).astype(f32)
    blocks = [tent_value(SHIFT_LOW + 2 * q + parity - offs, frac) / total for q in range(PAIRS)]
    sums = jnp.sum(sum(blocks)[:, :n], axis=1, keepdims=True) / n
    uniform = jnp.log(sums + pltpu.roll(jnp.broadcast_to(sums, (8, w)), 4, 0)[:, :1])
    faint = jnp.exp(-jnp.sum(sum(blocks) * uniform, axis=0, keepdims=True) / 4.0)
    both_high, back_low = [], []
    for block in blocks:
        high, low = split(block / 4.0)
        both_high += [high.astype(f32)] * 2
        back_low.append(low.astype(f32))
    stacked = jnp.concatenate(both_high + back_low + [jnp.zeros((40, w), f32)], axis=0)
    back_ref[...] = jnp.transpose(stacked)[:n, :224].astype(bf16)
    high, low = split(jnp.concatenate(blocks, axis=0) * (faint / n))
    forward_ref[...] = jnp.concatenate([high, low], axis=1)[:, : 3 * n]

    swap = lambda v: pltpu.roll(v, n, 1)

    def spread(pack_from, high_from, first_lane, count):
        pieces = [pack_from[:, pl.ds(first_lane + 2 * w * q, count)] for q in range(PAIRS)]
        pieces += [high_from[:, pl.ds(first_lane + 2 * w * q, count)] for q in range(0, PAIRS, 2)]
        return jnp.concatenate(pieces, axis=0)

    lo_x, hi_x = -REACH, n + REACH
    chunk = 100 * w
    back_w = back_ref[...]
    forward_w = forward_ref[...]

    def first_pass(i, _):
        start = pl.multiple_of(i * chunk, 2 * w)
        logv = dot(back_w, spread(pack_in_ref, high_in_ref, start + (lo_x + SHIFT_LOW + MARGIN) * w, chunk))
        high, low = split(jnp.exp(logv))
        shifted_ref[:, pl.ds(start, chunk)] = dot(forward_w, jnp.concatenate([high, low, high], axis=0))
        return 0

    lax.fori_loop(0, (hi_x - lo_x) * w // chunk, first_pass, 0)

    lo_u, hi_u = -10, n + 10
    count = (hi_u - lo_u) * w
    gathered = sum(
        shifted_ref[8 * q : 8 * q + 8, pl.ds((lo_u - SHIFT_LOW - 2 * q - lo_x) * w, count)] for q in range(PAIRS)
    )
    proj = gathered[:, 2 * w :] + pltpu.roll(gathered[:, w : count - w], 4, 0)
    ratio = first_ref[:, (lo_u + 2 + MARGIN) * w : (hi_u + MARGIN) * w]
    ratio = (ratio - uniform) + (ratio - jnp.log(proj))
    later = pltpu.roll(jnp.concatenate([ratio[:, w:], ratio[:, :w]], axis=1), 4, 0)
    pack(jnp.where(lax.broadcasted_iota(jnp.int32, ratio.shape, 0) < 4, ratio, later), pack_ref, high_ref)

    top = lax.broadcasted_iota(jnp.int32, (8, w), 0) == 0
    place = lambda x: jnp.where(x <= HALF, x, n + HALF - x)

    per = 64
    chunk2 = per * w

    def second_pass(i, _):
        start = pl.multiple_of(i * chunk2, chunk2)
        logv = dot(back_w, spread(pack_ref, high_ref, start, chunk2))
        high, low = split(jnp.exp(logv))
        spec = dot(z_fwd_ref[...], jnp.concatenate([high, low, high], axis=0))
        groups = []
        for j in range(per):
            piece = spec[:, w * j : w * (j + 1)]
            imag = jnp.concatenate([jnp.where(top, 0.0, piece[HALF : HALF + 8]), piece[HALF + 8 :]], axis=0)
            groups.append(jnp.concatenate([piece[:HALF], imag], axis=1))
            edge_ref[0, pl.ds(place(i * per + j), 1), :] = piece[HALF : HALF + 1]
        high, low = split(jnp.concatenate(groups, axis=0))
        lines = dot(jnp.concatenate([high, low, high], axis=1), y_fwd_ref[...])
        for j in range(per):
            at = pl.multiple_of(place(i * per + j) * ROWS, ROWS)
            spec_ref[0, pl.ds(at, HALF), :] = lines[j * HALF : (j + 1) * HALF, :w]
            spec_ref[1, pl.ds(at, HALF), :] = lines[j * HALF : (j + 1) * HALF, w:]
        return 0

    lax.fori_loop(0, n // per, second_pass, 0)
    high, low = split(jnp.concatenate([edge_ref[0], jnp.zeros((n, w), f32)], axis=1))
    lines = dot(jnp.concatenate([high, low, high], axis=1), y_fwd_ref[...])
    edge_ref[0], edge_ref[1] = lines[:, :w], lines[:, w:]

    lane = lax.broadcasted_iota(jnp.int32, (n, w), 1)
    row = lax.broadcasted_iota(jnp.int32, (n, w), 0)
    own_sign = jnp.where(exp_index == 0, 1.0, -1.0)
    exp_sign = jnp.where(lane < n, own_sign, -own_sign)
    anchor = (lane == 0) & (row == 0)

    def three(value):
        high, low = split(value)
        return jnp.concatenate([high, low, high], axis=0)

    def folded(pieces):
        value = jnp.concatenate(pieces, axis=1)
        return three(jnp.concatenate([value[:HALF] + value[HALF:], value[:HALF] - value[HALF:]], axis=0))

    def unfolded(both, sign):
        cos_re, cos_im, sin_re, sin_im = (both[r : r + HALF, c : c + w] for r in (0, HALF) for c in (0, w))
        re, re_mirror = cos_re - sin_im, cos_re + sin_im
        im, im_mirror = cos_im + sin_re, cos_im - sin_re
        if sign < 0:
            re, re_mirror, im, im_mirror = re_mirror, re, im_mirror, im
        pieces = []
        for plain, mirror, cos_part, sin_part in ((re, re_mirror, cos_re, sin_re), (im, im_mirror, cos_im, sin_im)):
            first = [jnp.where(top, cos_part[:8], plain[:8]), plain[8:]]
            pieces.append(jnp.concatenate(first + [jnp.where(top, sin_part[:8], mirror[:8]), mirror[8:]], axis=0))
        return pieces

    def columns_to_spectrum(i):
        for t in range(UNROLL):
            for odd in range(2):
                kz = i * (2 * UNROLL) + 2 * t + odd
                lines = [spec_ref[ri, pl.ds(kz, n, stride=ROWS), :] for ri in range(2)]
                freq_ref[t, odd, 0], freq_ref[t, odd, 1] = unfolded(dot(x_fwd_ref[...], folded(lines)), -1.0)

    def last_to_spectrum():
        freq_ref[0, 0, 0], freq_ref[0, 0, 1] = unfolded(dot(x_fwd_ref[...], folded([edge_ref[0], edge_ref[1]])), -1.0)
        freq_ref[0, 1] = jnp.zeros((2, n, w), f32)

    def spectrum_to_cross(holds_anchor, count=UNROLL):
        for t in range(count):
            re_a, im_a = freq_ref[t, 0, 0], freq_ref[t, 0, 1]
            re_b, im_b = freq_ref[t, 1, 0], freq_ref[t, 1, 1]
            re_one = jnp.where(lane < n, re_a, re_b)
            im_one = jnp.where(lane < n, im_a, im_b)
            re_two = swap(jnp.where(lane < n, re_b, re_a))
            im_two = swap(jnp.where(lane < n, im_b, im_a))
            cross_re = re_one * re_two + im_one * im_two
            cross_im = re_one * im_two - im_one * re_two
            power = cross_re * cross_re + cross_im * cross_im
            gain = lax.rsqrt(jnp.maximum(power, spectral_floor * spectral_floor))
            if holds_anchor and t == 0:
                gain = jnp.where(anchor, 0.0, gain)
            cross_re, cross_im = cross_re * gain, cross_im * (gain * exp_sign)
            cross_ref[t] = folded([cross_re, cross_im])

    def cross_to_wave(i, count=UNROLL):
        for t in range(count):
            at = i * UNROLL + t
            high, low = split(jnp.concatenate(unfolded(dot(x_fwd_ref[...], cross_ref[t]), 1.0), axis=1))
            wave_ref[0, pl.ds(pl.multiple_of(at * n, n), n), :] = high
            wave_ref[1, pl.ds(pl.multiple_of(at * n, n), n), :] = low

    def wave_to_line(i, count=UNROLL):
        rows = pl.ds(pl.multiple_of(i * (UNROLL * n), UNROLL * n), count * n)
        high, low = wave_ref[0, rows, :], wave_ref[1, rows, :]
        lines = dot(jnp.concatenate([high, low, high], axis=1), yi_ref[...])
        for t in range(count):
            to = pl.multiple_of((i * UNROLL + t) * GAP, 8)
            line_ref[0, pl.ds(to, n), :] = lines[t * n : (t + 1) * n, :w]
            line_ref[1, pl.ds(to, n), :] = lines[t * n : (t + 1) * n, w:]

    def spectra(i, _):
        wave_to_line(i - 3)
        cross_to_wave(i - 2)
        spectrum_to_cross(False)
        columns_to_spectrum(i)
        return 0

    shift_copy.wait()
    for x in range(n):
        place_ref[x] = place(lax.rem(shift_ref[0, 1] + (n + x), n))
    columns_to_spectrum(0)
    spectrum_to_cross(True)
    columns_to_spectrum(1)
    cross_to_wave(0)
    spectrum_to_cross(False)
    columns_to_spectrum(2)
    lax.fori_loop(3, STEPS, spectra, 0)
    wave_to_line(STEPS - 3)
    cross_to_wave(STEPS - 2)
    spectrum_to_cross(False)
    last_to_spectrum()
    wave_to_line(STEPS - 2)
    cross_to_wave(STEPS - 1)
    spectrum_to_cross(False, 1)
    wave_to_line(STEPS - 1)
    cross_to_wave(STEPS, 1)
    wave_to_line(STEPS, 1)

    lane = lax.broadcasted_iota(jnp.int32, (HALF, w), 1)
    x_per_step = 32
    x_per_copy = 4

    def planes(i, _):
        for t in range(x_per_step):
            pair = i * x_per_step + t
            cols = jnp.concatenate(
                [
                    jnp.concatenate([line_ref[ri, pl.ds(place_ref[2 * pair + p], GROUPS, stride=GAP), :] for ri in range(2)], axis=0)
                    for p in range(2)
                ],
                axis=1,
            )
            both = dot(zi_ref[...], three(cols))
            a_even, a_odd = both[:HALF, :w], both[:HALF, w:]
            b_even, b_odd = both[HALF:, :w], both[HALF:, w:]
            value = jnp.where(lane < n, a_even, b_odd) + swap(jnp.where(lane < n, a_odd, b_even))
            out_ref[:, pl.ds(pl.multiple_of(pair * w, w), w)] = value
            if t % x_per_copy == x_per_copy - 1:
                out_copy(i * (x_per_step // x_per_copy) + t // x_per_copy).start()
        return 0

    def out_copy(i):
        at = pl.ds(pl.multiple_of(i * (x_per_copy * w), x_per_copy * w), x_per_copy * w)
        return pltpu.make_async_copy(out_ref.at[:, at], out_hbm.at[:, at], out_sem.at[i])

    lax.fori_loop(0, HALF // x_per_step, planes, 0)
    for i in range(HALF // x_per_copy):
        out_copy(i).wait()


def table_kernel(offsets_ref, fractions_ref, out_ref):
    slab = offsets_ref.shape[1]
    width = out_ref.shape[1] // 2
    both = jnp.concatenate([offsets_ref[...].astype(f32), fractions_ref[...]], axis=0)
    wide = jnp.concatenate([both] * (2 * width // slab), axis=1)
    lane = lax.broadcasted_iota(jnp.int32, wide.shape, 1)
    out_ref[...] = jnp.where(lax.rem(lane, width) // slab == lax.axis_index("depth"), wide, 0.0)


def share_tables(offsets, fractions):
    vmem = pl.BlockSpec(memory_space=pltpu.VMEM)
    count = lax.axis_size("depth")
    cams, slab = offsets.shape
    table = pl.pallas_call(
        table_kernel,
        out_shape=jax.ShapeDtypeStruct((2 * cams, 2 * count * slab), f32),
        in_specs=[vmem] * 2,
        out_specs=vmem,
        compiler_params=pltpu.CompilerParams(vmem_limit_bytes=60 * 1024 * 1024),
    )(offsets, fractions)
    total = table
    for k in (1, 2, 3):
        total = total + lax.ppermute(table, "depth", [(i, i ^ k) for i in range(count)])
    table = total
    step = 4
    while step < count:
        table = table + lax.ppermute(table, "depth", [(i, i ^ step) for i in range(count)])
        step *= 2
    return table


def windows(images, bricks_x, bricks_y):
    exps, tiles, depths = (lax.axis_size(a) for a in ("exp", "tile", "depth"))
    depth_index = lax.axis_index("depth")
    cams = images.shape[1]
    strip = lax.dynamic_slice_in_dim(images[0], depth_index % bricks_y * BRICK, BRICK, axis=2).reshape(cams, -1)

    def linear(e, t, d):
        return ((e % exps) * tiles + t % tiles) * depths + d

    def edge(step, other):
        edge_part = 0 if step == 1 else bricks_x - 1
        return [
            (linear(e, t, d), linear(e + other, t + step, d))
            for e in range(exps)
            for t in range(tiles)
            for d in range(depths)
            if d // bricks_y == edge_part
        ]

    axes = ("exp", "tile", "depth")
    tail = strip[:, -MARGIN * BRICK :]
    head = strip[:, : MARGIN * BRICK]
    pads = []
    for other in (0, 1):
        if bricks_x > 1:
            sent = jnp.where(depth_index // bricks_y == 0, tail, head)
            pads.append(lax.ppermute(sent, axes, edge(1, other) + edge(-1, other))[None])
        else:
            sides = ((tail, 1), (head, -1))
            pads.append(jnp.stack([lax.ppermute(v, axes, edge(step, other)) for v, step in sides]))
    piece = strip
    if bricks_x == 2:
        near = strip.shape[1] - MARGIN * BRICK
        piece = jnp.where(depth_index // bricks_y == 0, strip[:, :near], strip[:, -near:])
    other_strip = lax.ppermute(piece, "exp", [(i, (i + 1) % exps) for i in range(exps)])
    return strip, other_strip, pads[0], pads[1]


def per_device(images, offsets, fractions, shifts):
    cams, width, rows_y = images.shape[1:]
    bricks_x, bricks_y = width // BRICK, rows_y // BRICK
    assert cams == 4 and width % BRICK == 0 and rows_y % BRICK == 0
    assert bricks_x * bricks_y == lax.axis_size("depth")
    assert offsets.shape[1] * lax.axis_size("depth") == BRICK
    n = BRICK
    table = share_tables(offsets, fractions)
    strips = windows(images, bricks_x, bricks_y)
    window = (n + 2 * MARGIN) * n
    extended = (width + 2 * MARGIN) * n
    vmem = pl.BlockSpec(memory_space=pltpu.VMEM)
    z_fwd, y_fwd, x_fwd, *inverses = (jnp.asarray(v) for v in constant_tables())
    turned = pl.pallas_call(
        turn,
        out_shape=[
            jax.ShapeDtypeStruct((12 * n, 4 * n), bf16),
            jax.ShapeDtypeStruct((n, 6 * GROUPS), bf16),
        ],
        in_specs=[pl.BlockSpec(memory_space=pltpu.SMEM)] + [vmem] * 2,
        out_specs=[vmem] * 2,
        compiler_params=pltpu.CompilerParams(vmem_limit_bytes=8 * 1024 * 1024),
    )(shifts, *inverses)
    ready = pl.pallas_call(
        functools.partial(prepare, bricks_y=bricks_y),
        out_shape=[
            jax.ShapeDtypeStruct((8, 2 * window), f32),
            jax.ShapeDtypeStruct((16, 2 * window), bf16),
            jax.ShapeDtypeStruct((16, 2 * window), bf16),
        ],
        in_specs=[vmem] * 4,
        out_specs=[vmem] * 3,
        scratch_shapes=[pltpu.VMEM((8, extended), f32)],
        compiler_params=pltpu.CompilerParams(vmem_limit_bytes=16 * 1024 * 1024),
    )(*strips)
    second = (n + 18) * 2 * n
    out = pl.pallas_call(
        kernel,
        out_shape=jax.ShapeDtypeStruct((HALF, n * n), f32),
        in_specs=[pl.BlockSpec(memory_space=pl.ANY)] + [vmem] * 9,
        out_specs=pl.BlockSpec(memory_space=pl.ANY),
        scratch_shapes=[
            pltpu.VMEM((16, second), bf16),
            pltpu.VMEM((16, second), bf16),
            pltpu.VMEM((8 * PAIRS, (n + 2 * REACH) * 2 * n), f32),
            pltpu.VMEM((2, n * ROWS, 2 * n), f32),
            pltpu.VMEM((2, n, 2 * n), f32),
            pltpu.VMEM((UNROLL, 2, 2, n, 2 * n), f32),
            pltpu.VMEM((UNROLL, 3 * n, 4 * n), bf16),
            pltpu.VMEM((2, PLANES * n, 4 * n), bf16),
            pltpu.VMEM((2, GROUPS * GAP, 2 * n), f32),
            pltpu.VMEM((n, 224), bf16),
            pltpu.VMEM((8 * PAIRS, 3 * n), bf16),
            pltpu.VMEM((HALF, n * n), f32),
            pltpu.SemaphoreType.DMA((8,)),
            pltpu.SMEM(shifts.shape, jnp.int32),
            pltpu.SemaphoreType.DMA(()),
            pltpu.SMEM((n,), jnp.int32),
        ],
        compiler_params=pltpu.CompilerParams(vmem_limit_bytes=40 * 1024 * 1024),
    )(shifts, table, *ready, *turned, z_fwd, y_fwd, x_fwd)
    return out.reshape(1, HALF, n * n)


def solution(mesh):
    placed = (
        P("exp", None, "tile", None),
        P(None, "depth"),
        P(None, "depth"),
        P(("tile", "depth"), None),
    )
    return jax.shard_map(
        per_device,
        mesh=mesh,
        in_specs=placed,
        out_specs=P(("tile", "depth"), "exp", None),
        check_vma=False,
    )
```
